32 devices in a mesh: fsdp: 32 (over z, y, x, core).
Axes of the slice: x: 2, y: 2, z: 4, core: 2. Of those that a mesh axis runs over, the one named last changes fastest.
Arguments:
- tokens: bfloat16 [2, 32, 576, 1024], P(None, 'fsdp'), may hold values from -5 to 5
- lengths: int32 [2, 32], P(None, 'fsdp'), may hold values from 196 to 576, as said below
- cotangent: float32 [2, 32, 8, 1024], P(None, 'fsdp'), may hold values from -768 to 768
- ln1_gain: bfloat16 [1024], P('fsdp'), may hold values from 0.5 to 1.5
- ln1_bias: bfloat16 [1024], P('fsdp'), may hold values from -1.1953125 to 1.1953125
- w_qkv: bfloat16 [1024, 3072], P('fsdp'), may hold values from -0.25 to 0.25
- b_qv: bfloat16 [2048], P('fsdp'), may hold values from -1.1953125 to 1.1953125
- w_out: bfloat16 [1024, 1024], P('fsdp'), may hold values from -0.375 to 0.375
- b_out: bfloat16 [1024], P('fsdp'), may hold values from -1.1953125 to 1.1953125
- ln2_gain: bfloat16 [1024], P('fsdp'), may hold values from 0.5 to 1.5
- ln2_bias: bfloat16 [1024], P('fsdp'), may hold values from -1.1953125 to 1.1953125
- w_up: bfloat16 [1024, 4096], P('fsdp'), may hold values from -0.1875 to 0.1875
- b_up: bfloat16 [4096], P('fsdp'), may hold values from -1.1953125 to 1.1953125
- w_down: bfloat16 [4096, 1024], P('fsdp'), may hold values from -0.09375 to 0.09375
- b_down: bfloat16 [1024], P('fsdp'), may hold values from -1.1953125 to 1.1953125
- ln3_gain: bfloat16 [1024], P('fsdp'), may hold values from 0.5 to 1.5
- ln3_bias: bfloat16 [1024], P('fsdp'), may hold values from -1.1953125 to 1.1953125
- w_learn: bfloat16 [1024, 1024], P('fsdp'), may hold values from -0.1875 to 0.1875
- b_learn: bfloat16 [1024], P('fsdp'), may hold values from -1.1953125 to 1.1953125
- w_map: bfloat16 [1024, 8], P('fsdp'), may hold values from -0.75 to 0.75
Outputs:
- pooled: float32 [2, 32, 8, 1024], P(None, 'fsdp')
- d_tokens: float32 [2, 32, 576, 1024], P(None, 'fsdp')
- grad_ln1_gain: float32 [1024], P('fsdp')
- grad_ln1_bias: float32 [1024], P('fsdp')
- grad_w_qkv: float32 [1024, 3072], P('fsdp')
- grad_b_qv: float32 [2048], P('fsdp')
- grad_w_out: float32 [1024, 1024], P('fsdp')
- grad_b_out: float32 [1024], P('fsdp')
- grad_ln2_gain: float32 [1024], P('fsdp')
- grad_ln2_bias: float32 [1024], P('fsdp')
- grad_w_up: float32 [1024, 4096], P('fsdp')
- grad_b_up: float32 [4096], P('fsdp')
- grad_w_down: float32 [4096, 1024], P('fsdp')
- grad_b_down: float32 [1024], P('fsdp')
- grad_ln3_gain: float32 [1024], P('fsdp')
- grad_ln3_bias: float32 [1024], P('fsdp')
- grad_w_learn: float32 [1024, 1024], P('fsdp')
- grad_b_learn: float32 [1024], P('fsdp')
- grad_w_map: float32 [1024, 8], P('fsdp')
The draws below stay inside these ranges and needn't reach their ends.
Inputs may be any that keep to these rules, and one draw needn't show every extreme that they name: `lengths`: each image has 196 or 576 patches; both counts occur in every draw.
All inputs are finite; a program needn't handle non-finite values.
Results may differ from the reference program's by a relative error of at most 0.013.
Values may be sent and summed in bfloat16 or wider, within the bound.
No kernel may reach another device: no remote copies, remote signals or barrier semaphores. Data moves between devices by JAX's collectives and lax.ppermute only.
A program may use at most 448 MiB of HBM per device.

```python
import jax
import jax.numpy as jnp
from jax import lax

D = 1024
HEADS = 16
HD = 64
FF = 4096
MAPS = 8
SLOTS = 576
SHORT = 196
MB = 2
IMAGES = 32


def draw_tokens(key, part):
    first = jax.random.fold_in(key, 11)
    second = jax.random.fold_in(key, 12)
    offset = jnp.clip(jax.random.normal(first, (MB, IMAGES, 1, D), jnp.float32), -3.0, 3.0)
    noise = jnp.clip(jax.random.normal(second, (MB, IMAGES, SLOTS, D), jnp.float32), -3.0, 3.0)
    return (0.2 * offset + noise).astype(jnp.bfloat16)


def draw_lengths(key, part):
    picks = jax.random.randint(jax.random.fold_in(key, 21), (MB, IMAGES), 0, 5)
    counts = jnp.where(picks < 2, SLOTS, SHORT).astype(jnp.int32)
    counts = counts.at[0, 0].set(SLOTS)
    counts = counts.at[0, 1].set(SHORT)
    return counts


def block_levels(key, shape, split, smallest, largest):
    def one(dim, shards_of):
        steps = jax.random.uniform(jax.random.fold_in(jax.random.fold_in(key, 6), dim), (shards_of,), jnp.float32, smallest / len(split), largest / len(split))
        return jnp.repeat(jnp.exp(steps), shape[dim] // shards_of).reshape((-1,) + (1,) * (len(shape) - dim - 1))

    factor_of = one(*split[0])
    for cut in split[1:]:
        factor_of = factor_of * one(*cut)
    return factor_of


def bell_draw(stream_key, shape, deviation, most, shards=(), kind=jnp.bfloat16):
    level = block_levels(stream_key, shape, shards, -0.22, 0.18) if shards else 1.0
    array = jax.random.normal(stream_key, shape, jnp.float32) * deviation * level
    return jnp.minimum(jnp.maximum(array, -most), most).astype(kind)


def setup_inputs(seed: int = 0) -> dict:
    key_list = jax.random.split(jax.random.key(seed), 21)
    tokens = draw_tokens(jax.random.fold_in(key_list[20], 71), 0)
    lengths = draw_lengths(jax.random.fold_in(key_list[20], 71), 0)
    cotangent = bell_draw(key_list[2], (MB, IMAGES, MAPS, D), 128.0, 768.0, ((1, 32),), jnp.float32)
    ln1_gain = jnp.clip(1.0 + 0.1 * jax.random.normal(key_list[3], (D,), jnp.float32), 0.5, 1.5).astype(jnp.bfloat16)
    ln1_bias = bell_draw(key_list[4], (D,), 0.2, 1.1953125, ((0, 32),))
    w_qkv = bell_draw(key_list[5], (D, 3 * D), (D // 2) ** -0.5, 0.25, ((0, 32),))
    b_qv = bell_draw(key_list[6], (2 * D,), 0.2, 1.1953125, ((0, 32),))
    w_out = bell_draw(key_list[7], (D, D), (D // 4) ** -0.5, 0.375, ((0, 32),))
    b_out = bell_draw(key_list[8], (D,), 0.2, 1.1953125, ((0, 32),))
    ln2_gain = jnp.clip(1.0 + 0.1 * jax.random.normal(key_list[9], (D,), jnp.float32), 0.5, 1.5).astype(jnp.bfloat16)
    ln2_bias = bell_draw(key_list[10], (D,), 0.2, 1.1953125, ((0, 32),))
    w_up = bell_draw(key_list[11], (D, FF), D ** -0.5, 0.1875, ((0, 32),))
    b_up = bell_draw(key_list[12], (FF,), 0.2, 1.1953125, ((0, 32),))
    w_down = bell_draw(key_list[13], (FF, D), FF ** -0.5, 0.09375, ((0, 32),))
    b_down = bell_draw(key_list[14], (D,), 0.2, 1.1953125, ((0, 32),))
    ln3_gain = jnp.clip(1.0 + 0.1 * jax.random.normal(key_list[15], (D,), jnp.float32), 0.5, 1.5).astype(jnp.bfloat16)
    ln3_bias = bell_draw(key_list[16], (D,), 0.2, 1.1953125, ((0, 32),))
    w_learn = bell_draw(key_list[17], (D, D), D ** -0.5, 0.1875, ((0, 32),))
    b_learn = bell_draw(key_list[18], (D,), 0.2, 1.1953125, ((0, 32),))
    w_map = bell_draw(key_list[19], (D, MAPS), (D // 16) ** -0.5, 0.75, ((0, 32),))
    return dict(tokens=tokens, lengths=lengths, cotangent=cotangent, ln1_gain=ln1_gain, ln1_bias=ln1_bias, w_qkv=w_qkv, b_qv=b_qv, w_out=w_out, b_out=b_out, ln2_gain=ln2_gain, ln2_bias=ln2_bias, w_up=w_up, b_up=b_up, w_down=w_down, b_down=b_down, ln3_gain=ln3_gain, ln3_bias=ln3_bias, w_learn=w_learn, b_learn=b_learn, w_map=w_map)


EPSILON = 1e-06
PRECISE = lax.Precision.HIGHEST

@jax.custom_vjp
def low(v):
    return lax.optimization_barrier(v.astype(jnp.bfloat16)).astype(jnp.float32)

@jax.custom_vjp
def low_back(v):
    return v

def low_keep(v):
    return (low(v), None)

def low_pass(kept, grad):
    return (grad,)

def back_keep(v):
    return (v, None)

def back_low(kept, grad):
    return (low(grad),)
low.defvjp(low_keep, low_pass)
low_back.defvjp(back_keep, back_low)

def layer_norm(values, gain, shift):
    row_mean = lax.optimization_barrier(jnp.mean(values, axis=-1, keepdims=True))
    centered = values - row_mean
    variance = lax.optimization_barrier(jnp.mean(centered * centered, axis=-1, keepdims=True))
    return centered * lax.rsqrt(variance + EPSILON) * gain + shift

def matmul(left, right):
    return jnp.dot(left, right, precision=PRECISE, preferred_element_type=jnp.float32)

def gelu_exact(values):
    return jax.nn.gelu(values, approximate=False)

def image_forward(params, image_rows, length):
    ln1_gain, ln1_bias, w_qkv, b_qv, w_out, b_out, ln2_gain, ln2_bias, w_up, b_up, w_down, b_down, ln3_gain, ln3_bias, w_learn, b_learn, w_map = params
    slot_count = image_rows.shape[0]
    slot_valid = jnp.arange(slot_count, dtype=jnp.int32) < length
    hidden = low(layer_norm(image_rows, ln1_gain, ln1_bias))
    qkv_rows = matmul(hidden, w_qkv)
    queries = low(low_back(qkv_rows[:, :D] + b_qv[:D])).reshape(slot_count, HEADS, HD)
    key_rows = low(low_back(qkv_rows[:, D:2 * D])).reshape(slot_count, HEADS, HD)
    values = low(low_back(qkv_rows[:, 2 * D:] + b_qv[D:])).reshape(slot_count, HEADS, HD)
    scores = low_back(jnp.einsum('qhd,khd->hqk', queries, key_rows, precision=PRECISE) * HD ** (-0.5))
    scores = jnp.where(slot_valid[None, None, :], scores, -1e+30)
    probs_low = low(jax.nn.softmax(scores, axis=-1))
    attended = jnp.einsum('hqk,khd->qhd', probs_low, values, precision=PRECISE).reshape(slot_count, D)
    attended = low(low_back(attended))
    branch = low_back(matmul(attended, w_out) + b_out)
    middle = image_rows + branch
    normed = low(layer_norm(middle, ln2_gain, ln2_bias))
    up_proj = low_back(matmul(normed, w_up) + b_up)
    up_act = low(gelu_exact(up_proj))
    mlp_out = low_back(matmul(up_act, w_down) + b_down)
    output = middle + mlp_out
    learn_in = low(layer_norm(output, ln3_gain, ln3_bias))
    learn_mid = low_back(matmul(learn_in, w_learn) + b_learn)
    learn_act = low(gelu_exact(learn_mid))
    logits = low_back(matmul(learn_act, w_map))
    pool_share = slot_valid.astype(jnp.float32) / length.astype(jnp.float32)
    pool_maps = jax.nn.sigmoid(logits) * pool_share[:, None]
    return jnp.einsum('sm,sd->md', pool_maps, output, precision=PRECISE)

def reference(tokens, lengths, cotangent, ln1_gain, ln1_bias, w_qkv, b_qv, w_out, b_out, ln2_gain, ln2_bias, w_up, b_up, w_down, b_down, ln3_gain, ln3_bias, w_learn, b_learn, w_map):
    params = tuple((item.astype(jnp.float32) for item in (ln1_gain, ln1_bias, w_qkv, b_qv, w_out, b_out, ln2_gain, ln2_bias, w_up, b_up, w_down, b_down, ln3_gain, ln3_bias, w_learn, b_learn, w_map)))
    flat_tokens = tokens.astype(jnp.float32).reshape(MB * IMAGES, SLOTS, D)
    flat_lengths = lengths.reshape(MB * IMAGES).astype(jnp.int32)
    flat_cot = cotangent.astype(jnp.float32).reshape(MB * IMAGES, MAPS, D)

    def forward(param_set, images):

        def single(item_pack):
            return jax.checkpoint(image_forward)(param_set, item_pack[0], item_pack[1])
        return lax.map(single, (images, flat_lengths))
    pooled, pull_back = jax.vjp(forward, params, flat_tokens)
    grad_set, d_flat = pull_back(flat_cot)
    return (pooled.reshape(MB, IMAGES, MAPS, D), d_flat.reshape(MB, IMAGES, SLOTS, D), grad_set[0], grad_set[1], grad_set[2], grad_set[3], grad_set[4], grad_set[5], grad_set[6], grad_set[7], grad_set[8], grad_set[9], grad_set[10], grad_set[11], grad_set[12], grad_set[13], grad_set[14], grad_set[15], grad_set[16])
```

```python
import functools

import jax
import jax.numpy as jnp
from jax import lax
from jax.experimental import pallas as pl
from jax.experimental.pallas import tpu as pltpu
from jax.sharding import PartitionSpec as P

D = 1024
HEADS = 16
HD = 64
PAIR = 2 * HD
EPSILON = 1e-06
SCALE = 0.125
LOG2E = 1.4426950408889634
SHORT_ROWS = 256
PAIRS = 2
BF = jnp.bfloat16
F32 = jnp.float32

NN = (((1,), (0,)), ((), ()))
NT = (((1,), (1,)), ((), ()))
TN = (((0,), (0,)), ((), ()))


def mm(left, right, dims):
    return lax.dot_general(left, right, dims, preferred_element_type=F32)


def layer_norm_parts(values):
    row_mean = jnp.mean(values, axis=-1, keepdims=True)
    centered = values - row_mean
    variance = jnp.mean(centered * centered, axis=-1, keepdims=True)
    rstd = lax.rsqrt(variance + EPSILON)
    return centered * rstd, rstd


def layer_norm(values, gain, shift):
    return layer_norm_parts(values)[0] * gain + shift


def norm_back(values, gain, incoming):
    normed, rstd = layer_norm_parts(values)
    scaled = incoming * gain
    grad = rstd * (
        scaled
        - jnp.mean(scaled, axis=-1, keepdims=True)
        - normed * jnp.mean(scaled * normed, axis=-1, keepdims=True)
    )
    return grad, jnp.sum(incoming * normed, axis=0), jnp.sum(incoming, axis=0)


def gelu_exact(values):
    return jax.nn.gelu(values, approximate=False)


def gelu_pair(values):
    half = 0.5 * lax.erfc(-values * (0.5**0.5))
    slope = half + values * (jnp.exp(-0.5 * values * values) * 0.3989422804014327)
    return values * half, slope


def head_lanes(shape, head):
    return (lax.broadcasted_iota(jnp.int32, shape, 1) // HD) == head


def key_mask(scores, length):
    return jnp.where(lax.broadcasted_iota(jnp.int32, scores.shape, 0) < length, scores, -1e30)


def attention_forward_kernel(slots, len_ref, q_ref, k_ref, v_ref, o_ref, lse_ref):
    length = len_ref[pl.program_id(0)]

    def attend(rows, masked):
        for pair in range(PAIRS):
            lanes = pl.ds(pair * PAIR, PAIR)
            q = q_ref[:rows, lanes]
            k = k_ref[:rows, lanes]
            v_t = v_ref[:rows, lanes].T
            outs = []
            for head in range(2):
                q_one = jnp.where(head_lanes(q.shape, head), q, jnp.zeros_like(q))
                scores = mm(k, q_one, NT)
                if masked:
                    scores = key_mask(scores, length)
                top = jnp.max(scores, axis=0, keepdims=True)
                probs = jnp.exp2((scores - top) * (SCALE * LOG2E))
                total = jnp.sum(probs, axis=0, keepdims=True)
                out = mm(v_t[head * HD : (head + 1) * HD], probs.astype(BF), NN)
                outs.append(out * (1.0 / total))
                lse_ref[0, pair * 2 + head : pair * 2 + head + 1, :rows] = top * (
                    SCALE * LOG2E
                ) + jnp.log2(total)
            o_ref[:rows, lanes] = jnp.concatenate(outs, 0).astype(BF).T

    @pl.when(length > SHORT_ROWS)
    def _():
        attend(slots, False)

    @pl.when(length <= SHORT_ROWS)
    def _():
        o_ref[...] = jnp.zeros_like(o_ref)
        lse_ref[...] = jnp.zeros_like(lse_ref)
        attend(SHORT_ROWS, True)


def attention_backward_kernel(
    slots, len_ref, q_ref, k_ref, v_ref, o_ref, do_ref, lse_ref, dq_ref, dk_ref, dv_ref
):
    length = len_ref[pl.program_id(0)]

    def attend(rows, masked):
        for pair in range(PAIRS):
            lanes = pl.ds(pair * PAIR, PAIR)
            q = q_ref[:rows, lanes]
            k = k_ref[:rows, lanes]
            v = v_ref[:rows, lanes]
            do = do_ref[:rows, lanes]
            weighted = o_ref[:rows, lanes].astype(F32) * do.astype(F32)
            k_t = k.T
            zero = jnp.zeros_like(q)
            dqs = []
            dks = []
            dvs = []
            for head in range(2):
                own = head_lanes(q.shape, head)
                ones = jnp.where(head_lanes((8, PAIR), head), 1.0, 0.0)
                row_dot = lax.dot_general(
                    ones, weighted, NT, precision=lax.Precision.HIGHEST, preferred_element_type=F32
                )[0:1]
                scores = mm(k, jnp.where(own, q, zero), NT)
                if masked:
                    scores = key_mask(scores, length)
                lse = lse_ref[0, pair * 2 + head : pair * 2 + head + 1, :rows]
                probs = jnp.exp2(scores * (SCALE * LOG2E) - lse)
                d_probs = mm(v, jnp.where(own, do, zero), NT)
                d_scores = (probs * (d_probs - row_dot)).astype(BF)
                dvs.append(mm(probs.astype(BF), do, NN))
                dks.append(mm(d_scores, q, NN))
                dqs.append(mm(k_t[head * HD : (head + 1) * HD], d_scores, NN))
            low = head_lanes(dks[0].shape, 0)
            dv_ref[:rows, lanes] = jnp.where(low, dvs[0], dvs[1]).astype(BF)
            dk_ref[:rows, lanes] = (jnp.where(low, dks[0], dks[1]) * SCALE).astype(BF)
            dq_ref[:rows, lanes] = (jnp.concatenate(dqs, 0) * SCALE).astype(BF).T

    @pl.when(length > SHORT_ROWS)
    def _():
        attend(slots, False)

    @pl.when(length <= SHORT_ROWS)
    def _():
        for ref in (dq_ref, dk_ref, dv_ref):
            ref[...] = jnp.zeros_like(ref)
        attend(SHORT_ROWS, True)


def head_blocks(slots, part):
    steps = HEADS // (2 * PAIRS)
    return pl.BlockSpec((slots, PAIRS * PAIR), lambda b, h, lens: (b, part * steps + h))


def lse_blocks(slots):
    steps = HEADS // (2 * PAIRS)
    return pl.BlockSpec((1, 2 * PAIRS, slots), lambda b, h, lens: (b * steps + h, 0, 0))


def attention_forward(qkv, lengths):
    images = lengths.shape[0]
    slots = qkv.shape[0] // images
    steps = HEADS // (2 * PAIRS)
    return pl.pallas_call(
        functools.partial(attention_forward_kernel, slots),
        out_shape=(
            jax.ShapeDtypeStruct((images * slots, D), BF),
            jax.ShapeDtypeStruct((images * steps, 2 * PAIRS, slots), F32),
        ),
        grid_spec=pltpu.PrefetchScalarGridSpec(
            num_scalar_prefetch=1,
            grid=(images, steps),
            in_specs=[head_blocks(slots, 0), head_blocks(slots, 1), head_blocks(slots, 2)],
            out_specs=(head_blocks(slots, 0), lse_blocks(slots)),
        ),
        name="attention_forward",
    )(lengths, qkv, qkv, qkv)


def attention_backward(qkv, attended, d_attended, lse, lengths):
    images = lengths.shape[0]
    slots = qkv.shape[0] // images
    steps = HEADS // (2 * PAIRS)
    first = head_blocks(slots, 0)
    return pl.pallas_call(
        functools.partial(attention_backward_kernel, slots),
        out_shape=tuple(jax.ShapeDtypeStruct((images * slots, D), BF) for _ in range(3)),
        grid_spec=pltpu.PrefetchScalarGridSpec(
            num_scalar_prefetch=1,
            grid=(images, steps),
            in_specs=[
                first,
                head_blocks(slots, 1),
                head_blocks(slots, 2),
                first,
                first,
                lse_blocks(slots),
            ],
            out_specs=(first, first, first),
        ),
        name="attention_backward",
    )(lengths, qkv, qkv, qkv, attended, d_attended, lse)


def gather(shard):
    return lax.all_gather(shard, "fsdp", axis=0, tiled=True)


def scatter_sum(grad):
    return lax.psum_scatter(grad.astype(BF), "fsdp", scatter_dimension=0, tiled=True).astype(F32)


def columns(vector, rows):
    return vector.reshape(-1, rows).T


def body(
    tokens,
    lengths,
    cotangent,
    ln1_gain,
    ln1_bias,
    w_qkv,
    b_qv,
    w_out,
    b_out,
    ln2_gain,
    ln2_bias,
    w_up,
    b_up,
    w_down,
    b_down,
    ln3_gain,
    ln3_bias,
    w_learn,
    b_learn,
    w_map,
):
    micro, local, slots, _ = tokens.shape
    images = micro * local
    shard_rows = w_qkv.shape[0]
    devices = D // shard_rows
    vectors = (
        ln1_gain, ln1_bias, b_out, ln2_gain, ln2_bias, b_down, ln3_gain, ln3_bias, b_learn, b_qv, b_up,
    )
    small = jnp.concatenate([columns(item, shard_rows) for item in vectors] + [w_map], axis=1)
    small_count = small.shape[1]
    pad = (-small_count) % 128
    first = gather(jnp.concatenate([w_qkv, jnp.pad(small, ((0, 0), (0, pad)))], axis=1))
    w_qkv = first[:, : 3 * D]
    spread = first[:, 3 * D : 3 * D + small_count]
    lines = spread.reshape(devices, shard_rows, small_count).transpose(2, 0, 1)
    named = []
    offset = 0
    for item in vectors:
        count = item.shape[0] // shard_rows
        part = lines[offset : offset + count].transpose(1, 0, 2).reshape(1, -1)
        named.append(part.astype(F32))
        offset = offset + count
    (ln1_gain, ln1_bias, b_out, ln2_gain, ln2_bias, b_down, ln3_gain, ln3_bias, b_learn, b_qv, b_up) = named
    w_map = spread[:, offset:]
    w_out = gather(w_out)
    w_up = gather(w_up)
    w_down = gather(w_down)
    w_learn = gather(w_learn)

    lengths = lengths.reshape(images)
    row_total = images * slots
    source = tokens.reshape(row_total, D).astype(F32)
    hidden = layer_norm(source, ln1_gain, ln1_bias).astype(BF)
    qkv_bias = jnp.concatenate([b_qv[:, :D], jnp.zeros((1, D), F32), b_qv[:, D:]], axis=1)
    qkv = (mm(hidden, w_qkv, NN) + qkv_bias).astype(BF)
    attended, lse = attention_forward(qkv, lengths)
    middle = source + mm(attended, w_out, NN) + b_out
    normed = layer_norm(middle, ln2_gain, ln2_bias).astype(BF)
    up_act, up_slope = gelu_pair(mm(normed, w_up, NN) + b_up)
    up_act = up_act.astype(BF)
    up_slope = up_slope.astype(BF)
    output = middle + mm(up_act, w_down, NN) + b_down
    learn_in = layer_norm(output, ln3_gain, ln3_bias).astype(BF)
    learn_act, learn_slope = gelu_pair(mm(learn_in, w_learn, NN) + b_learn)
    learn_act = learn_act.astype(BF)
    learn_slope = learn_slope.astype(BF)
    logits = mm(learn_act, w_map, NN)
    slot_valid = lax.broadcasted_iota(jnp.int32, (images, slots, 1), 1) < lengths[:, None, None]
    pool_share = (slot_valid.astype(F32) / lengths[:, None, None].astype(F32)).reshape(row_total, 1)
    squashed = jax.nn.sigmoid(logits)
    pool_maps = (squashed * pool_share).reshape(images, slots, -1)
    by_image = output.reshape(images, slots, D)
    pooled = jnp.einsum("bsm,bsd->bmd", pool_maps, by_image, precision=lax.Precision.HIGHEST)
    pool_grad = cotangent.reshape(images, -1, D)
    d_maps = jnp.einsum("bsd,bmd->bsm", by_image, pool_grad, precision=lax.Precision.HIGHEST)
    d_maps = d_maps.reshape(row_total, -1)
    d_output = jnp.einsum("bsm,bmd->bsd", pool_maps, pool_grad, precision=lax.Precision.HIGHEST)
    d_output = d_output.reshape(row_total, D)
    d_logits = (d_maps * pool_share * squashed * (1.0 - squashed)).astype(BF)
    g_map = mm(learn_act, d_logits, TN)
    d_learn = (learn_slope.astype(F32) * mm(d_logits, w_map, NT)).astype(BF)
    g_blearn = jnp.sum(d_learn.astype(F32), axis=0)
    g_wlearn = scatter_sum(mm(learn_in, d_learn, TN))
    d_norm3, g_ln3, h_ln3 = norm_back(output, ln3_gain, mm(d_learn, w_learn, NT))
    d_output = d_output + d_norm3
    d_mlp = d_output.astype(BF)
    g_bdown = jnp.sum(d_mlp.astype(F32), axis=0)
    g_wdown = scatter_sum(mm(up_act, d_mlp, TN))
    d_up = (up_slope.astype(F32) * mm(d_mlp, w_down, NT)).astype(BF)
    g_bup = jnp.sum(d_up.astype(F32), axis=0)
    g_wup = scatter_sum(mm(normed, d_up, TN))
    d_norm2, g_ln2, h_ln2 = norm_back(middle, ln2_gain, mm(d_up, w_up, NT))
    d_middle = d_output + d_norm2
    d_branch = d_middle.astype(BF)
    g_bout = jnp.sum(d_branch.astype(F32), axis=0)
    g_wout = scatter_sum(mm(attended, d_branch, TN))
    d_attended = mm(d_branch, w_out, NT).astype(BF)
    d_queries, d_keys, d_values = attention_backward(qkv, attended, d_attended, lse, lengths)
    d_qkv = jnp.concatenate([d_queries, d_keys, d_values], axis=1)
    g_bqv = jnp.concatenate(
        [jnp.sum(d_queries.astype(F32), axis=0), jnp.sum(d_values.astype(F32), axis=0)]
    )
    g_wqkv = mm(hidden, d_qkv, TN)
    d_norm1, g_ln1, h_ln1 = norm_back(source, ln1_gain, mm(d_qkv, w_qkv, NT))
    d_image = (d_middle + d_norm1).reshape(tokens.shape)

    grads = (g_ln1, h_ln1, g_bout, g_ln2, h_ln2, g_bdown, g_ln3, h_ln3, g_blearn, g_bqv, g_bup)
    spread = jnp.concatenate(
        [item.reshape(devices, -1, shard_rows).transpose(0, 2, 1).reshape(D, -1) for item in grads]
        + [g_map, jnp.zeros((D, pad), F32)],
        axis=1,
    )
    last = scatter_sum(jnp.concatenate([g_wqkv, spread], axis=1))
    small = last[:, 3 * D :]
    outs = []
    offset = 0
    for item in vectors:
        count = item.shape[0] // shard_rows
        outs.append(small[:, offset : offset + count].T.reshape(-1))
        offset = offset + count
    (g_ln1, h_ln1, g_bout, g_ln2, h_ln2, g_bdown, g_ln3, h_ln3, g_blearn, g_bqv, g_bup) = outs
    g_map = small[:, offset:small_count]
    pooled = pooled.reshape(cotangent.shape)
    return (
        pooled, d_image, g_ln1, h_ln1, last[:, : 3 * D], g_bqv, g_wout, g_bout, g_ln2, h_ln2,
        g_wup, g_bup, g_wdown, g_bdown, g_ln3, h_ln3, g_wlearn, g_blearn, g_map,
    )


def solution(mesh):
    rows = P("fsdp", None)
    line = P("fsdp")
    batch = P(None, "fsdp", None, None)
    params = (line, line, rows, line, rows, line, line, line, rows, line, rows, line, line, line, rows, line, rows)
    return jax.shard_map(
        body,
        mesh=mesh,
        in_specs=(batch, P(None, "fsdp"), batch) + params,
        out_specs=(batch, batch) + params,
        check_vma=False,
    )
```

```python
import functools

import jax
import jax.numpy as jnp
from jax import lax
from jax.experimental import pallas as pl
from jax.experimental.pallas import tpu as pltpu
from jax.sharding import PartitionSpec as P

D = 1024
HEADS = 16
HD = 64
PAIR = 2 * HD
EPSILON = 1e-06
SCALE = 0.125
LOG2E = 1.4426950408889634
SHORT_ROWS = 256
PAIRS = 2
BF = jnp.bfloat16
F32 = jnp.float32

NN = (((1,), (0,)), ((), ()))
NT = (((1,), (1,)), ((), ()))
TN = (((0,), (0,)), ((), ()))


def mm(left, right, dims):
    return lax.dot_general(left, right, dims, preferred_element_type=F32)


def layer_norm_parts(values):
    row_mean = jnp.mean(values, axis=-1, keepdims=True)
    centered = values - row_mean
    variance = jnp.mean(centered * centered, axis=-1, keepdims=True)
    rstd = lax.rsqrt(variance + EPSILON)
    return centered * rstd, rstd


def layer_norm(values, gain, shift):
    return layer_norm_parts(values)[0] * gain + shift


def norm_back(values, gain, incoming):
    normed, rstd = layer_norm_parts(values)
    scaled = incoming * gain
    grad = rstd * (
        scaled
        - jnp.mean(scaled, axis=-1, keepdims=True)
        - normed * jnp.mean(scaled * normed, axis=-1, keepdims=True)
    )
    return grad, jnp.sum(incoming * normed, axis=0), jnp.sum(incoming, axis=0)


ERFCX = (
    0.18636609783492827,
    0.1828374067871815,
    0.2019228837403338,
    0.045013532984771946,
    0.4125364399329413,
    -0.3554335531070661,
    0.46268519224041466,
    -0.13592808196895617,
)
ERFCX_SCALE = 0.33


def gelu_with_slope(values):
    near = 1.0 / (1.0 + jnp.abs(values) * (ERFCX_SCALE * 0.5**0.5))
    series = 0.5 * ERFCX[-1] * near + 0.5 * ERFCX[-2]
    for item in ERFCX[-3::-1]:
        series = series * near + 0.5 * item
    bell = jnp.exp2((values * values) * (-0.5 * LOG2E))
    tail = (bell * near) * series
    half = jnp.where(values < 0, tail, 1.0 - tail)
    return values * half, half + values * (bell * 0.3989422804014327)


def gelu_matmul_kernel(chunk, tiles, x_ref, b_ref, *refs):
    w_refs = refs[: len(tiles)]
    act_ref, slope_ref = refs[len(tiles) :]
    step = pl.program_id(0)
    first = 0
    for w_ref, count in zip(w_refs, tiles):

        @pl.when((step >= first) & (step < first + count))
        def _(w_ref=w_ref):
            for start in range(0, x_ref.shape[0], chunk):
                rows = pl.ds(start, chunk)
                act, slope = gelu_with_slope(mm(x_ref[rows], w_ref[...], NN) + b_ref[...])
                act_ref[rows] = act.astype(BF)
                slope_ref[rows] = slope.astype(BF)

        first = first + count


def slope_matmul_kernel(chunk, x_ref, w_ref, slope_ref, out_ref, sum_ref):
    total = jnp.zeros(sum_ref.shape, F32)
    for start in range(0, x_ref.shape[0], chunk):
        rows = pl.ds(start, chunk)
        out = (mm(x_ref[rows], w_ref[...], NT) * slope_ref[rows].astype(F32)).astype(BF)
        out_ref[rows] = out
        total = total + jnp.sum(out.astype(F32), axis=0, keepdims=True)
    sum_ref[...] = total


def light():
    return pl.CostEstimate(flops=1024, bytes_accessed=1024, transcendentals=0)


def gelu_matmul(x, pieces, bias):
    rows, inner = x.shape
    tile = 512
    width = bias.shape[1]
    tiles = [item[2] // tile for item in pieces]
    specs = []
    before = 0
    for (_, first, _), count in zip(pieces, tiles):

        def place(j, first=first, before=before, count=count):
            return 0, first // tile + jnp.clip(j - before, 0, count - 1)

        specs.append(pl.BlockSpec((inner, tile), place))
        before = before + count
    out = pl.BlockSpec((rows, tile), lambda j: (0, j))
    return pl.pallas_call(
        functools.partial(gelu_matmul_kernel, rows // 4, tiles),
        out_shape=(jax.ShapeDtypeStruct((rows, width), BF),) * 2,
        grid=(width // tile,),
        in_specs=[pl.BlockSpec((rows, inner), lambda j: (0, 0)), pl.BlockSpec((1, tile), lambda j: (0, j))] + specs,
        out_specs=(out, out),
        cost_estimate=light(),
        name="gelu_matmul",
    )(x, bias, *[item[0] for item in pieces])


def back_product_kernel(count, *refs):
    total = mm(refs[0][...], refs[count][...], NT)
    for i in range(1, count):
        total = total + mm(refs[i][...], refs[count + i][...], NT)
    refs[-1][...] = total


def back_product(pieces, w):
    count = len(pieces)
    rows, width = pieces[0].shape
    height = w.shape[0]
    tile = 512
    whole = pl.BlockSpec((rows, width), lambda j: (0, 0))
    parts = [pl.BlockSpec((tile, width), lambda j, i=i: (j, i)) for i in range(count)]
    return pl.pallas_call(
        functools.partial(back_product_kernel, count),
        out_shape=jax.ShapeDtypeStruct((rows, height), F32),
        grid=(height // tile,),
        in_specs=[whole] * count + parts,
        out_specs=pl.BlockSpec((rows, tile), lambda j: (0, j)),
        cost_estimate=light(),
        name="back_product",
    )(*pieces, *[w] * count)


def slope_matmul(x, w, slope):
    rows, inner = x.shape
    width = w.shape[0]
    tile = 1024
    block = pl.BlockSpec((rows, tile), lambda j: (0, j))
    return pl.pallas_call(
        functools.partial(slope_matmul_kernel, rows // 4),
        out_shape=(jax.ShapeDtypeStruct((rows, width), BF), jax.ShapeDtypeStruct((1, width), F32)),
        grid=(width // tile,),
        in_specs=[
            pl.BlockSpec((rows, inner), lambda j: (0, 0)),
            pl.BlockSpec((tile, inner), lambda j: (j, 0)),
            block,
        ],
        out_specs=(block, pl.BlockSpec((1, tile), lambda j: (0, j))),
        cost_estimate=light(),
        name="slope_matmul",
    )(x, w, slope)


def head_lanes(shape, head):
    return (lax.broadcasted_iota(jnp.int32, shape, 1) // HD) == head


def key_mask(scores, length):
    return jnp.where(lax.broadcasted_iota(jnp.int32, scores.shape, 0) < length, scores, -1e30)


def attention_forward_kernel(slots, image, len_ref, q_ref, k_ref, v_ref, o_ref, lse_ref):
    length = len_ref[image]

    def attend(rows, masked):
        for pair in range(PAIRS):
            lanes = pl.ds(pair * PAIR, PAIR)
            q = q_ref[:rows, lanes]
            k = k_ref[:rows, lanes]
            v_t = v_ref[:rows, lanes].T
            outs = []
            for head in range(2):
                q_one = jnp.where(head_lanes(q.shape, head), q, jnp.zeros_like(q))
                scores = mm(k, q_one, NT)
                if masked:
                    scores = key_mask(scores, length)
                top = jnp.max(scores, axis=0, keepdims=True)
                probs = jnp.exp2((scores - top) * (SCALE * LOG2E))
                total = jnp.sum(probs, axis=0, keepdims=True)
                out = mm(v_t[head * HD : (head + 1) * HD], probs.astype(BF), NN)
                outs.append(out * (1.0 / total))
                lse_ref[0, pair * 2 + head : pair * 2 + head + 1, :rows] = top * (
                    SCALE * LOG2E
                ) + jnp.log2(total)
            o_ref[:rows, lanes] = jnp.concatenate(outs, 0).astype(BF).T

    @pl.when(length > SHORT_ROWS)
    def _():
        attend(slots, False)

    @pl.when(length <= SHORT_ROWS)
    def _():
        o_ref[...] = jnp.zeros_like(o_ref)
        lse_ref[...] = jnp.zeros_like(lse_ref)
        attend(SHORT_ROWS, True)


def attention_backward_kernel(
    slots, image, len_ref, q_ref, k_ref, v_ref, o_ref, do_ref, lse_ref, dq_ref, dk_ref, dv_ref
):
    length = len_ref[image]

    def attend(rows, masked):
        for pair in range(PAIRS):
            lanes = pl.ds(pair * PAIR, PAIR)
            q = q_ref[:rows, lanes]
            k = k_ref[:rows, lanes]
            v = v_ref[:rows, lanes]
            do = do_ref[:rows, lanes]
            weighted = o_ref[:rows, lanes].astype(F32) * do.astype(F32)
            k_t = k.T
            zero = jnp.zeros_like(q)
            dqs = []
            dks = []
            dvs = []
            for head in range(2):
                own = head_lanes(q.shape, head)
                ones = jnp.where(head_lanes((8, PAIR), head), 1.0, 0.0)
                row_dot = lax.dot_general(
                    ones, weighted, NT, precision=lax.Precision.HIGHEST, preferred_element_type=F32
                )[0:1]
                scores = mm(k, jnp.where(own, q, zero), NT)
                if masked:
                    scores = key_mask(scores, length)
                lse = lse_ref[0, pair * 2 + head : pair * 2 + head + 1, :rows]
                probs = jnp.exp2(scores * (SCALE * LOG2E) - lse)
                d_probs = mm(v, jnp.where(own, do, zero), NT)
                d_scores = (probs * (d_probs - row_dot)).astype(BF)
                dvs.append(mm(probs.astype(BF), do, NN))
                dks.append(mm(d_scores, q, NN))
                dqs.append(mm(k_t[head * HD : (head + 1) * HD], d_scores, NN))
            low = head_lanes(dks[0].shape, 0)
            dv_ref[:rows, lanes] = jnp.where(low, dvs[0], dvs[1]).astype(BF)
            dk_ref[:rows, lanes] = (jnp.where(low, dks[0], dks[1]) * SCALE).astype(BF)
            dq_ref[:rows, lanes] = (jnp.concatenate(dqs, 0) * SCALE).astype(BF).T

    @pl.when(length > SHORT_ROWS)
    def _():
        attend(slots, False)

    @pl.when(length <= SHORT_ROWS)
    def _():
        for ref in (dq_ref, dk_ref, dv_ref):
            ref[...] = jnp.zeros_like(ref)
        attend(SHORT_ROWS, True)


def head_blocks(slots, image, part=0):
    first = part * (HEADS // (2 * PAIRS))
    return pl.BlockSpec((slots, PAIRS * PAIR), lambda h, lens: (image, first + h))


def lse_blocks(slots, image):
    steps = HEADS // (2 * PAIRS)
    return pl.BlockSpec((1, 2 * PAIRS, slots), lambda h, lens: (image * steps + h, 0, 0))


def held_in_place(kernel, count):
    def whole(len_ref, *refs):
        return kernel(len_ref, *refs[count:])

    return whole


def attention_forward(image, qkv, lengths, filled):
    images = lengths.shape[0]
    slots = qkv.shape[0] // images
    steps = HEADS // (2 * PAIRS)
    block = head_blocks(slots, image)
    outs = (block, lse_blocks(slots, image))
    kernel = functools.partial(attention_forward_kernel, slots, image)
    anywhere = [pl.BlockSpec(memory_space=pl.ANY)] * len(filled)
    return pl.pallas_call(
        held_in_place(kernel, len(filled)),
        out_shape=(
            jax.ShapeDtypeStruct((images * slots, D), BF),
            jax.ShapeDtypeStruct((images * steps, 2 * PAIRS, slots), F32),
        ),
        grid_spec=pltpu.PrefetchScalarGridSpec(
            num_scalar_prefetch=1,
            grid=(steps,),
            in_specs=anywhere + [head_blocks(slots, image, part) for part in range(3)],
            out_specs=outs,
        ),
        input_output_aliases={1 + i: i for i in range(len(filled))},
        cost_estimate=light(),
        name="attention_forward",
    )(lengths, *filled, qkv, qkv, qkv)


def attention_backward(image, qkv, attended, d_attended, lse, lengths, filled):
    images = lengths.shape[0]
    slots = qkv.shape[0] // images
    steps = HEADS // (2 * PAIRS)
    block = head_blocks(slots, image)
    kernel = functools.partial(attention_backward_kernel, slots, image)
    anywhere = [pl.BlockSpec(memory_space=pl.ANY)] * len(filled)
    return pl.pallas_call(
        held_in_place(kernel, len(filled)),
        out_shape=tuple(jax.ShapeDtypeStruct((images * slots, D), BF) for _ in range(3)),
        grid_spec=pltpu.PrefetchScalarGridSpec(
            num_scalar_prefetch=1,
            grid=(steps,),
            in_specs=anywhere
            + [head_blocks(slots, image, part) for part in range(3)]
            + [block] * 2
            + [lse_blocks(slots, image)],
            out_specs=(block, block, block),
        ),
        input_output_aliases={1 + i: i for i in range(len(filled))},
        cost_estimate=light(),
        name="attention_backward",
    )(lengths, *filled, qkv, qkv, qkv, attended, d_attended, lse)


def gather(shard):
    return lax.all_gather(shard, "fsdp", axis=0, tiled=True)


def scatter_sum(grad):
    return lax.psum_scatter(grad.astype(BF), "fsdp", scatter_dimension=0, tiled=True).astype(F32)


def bit_value(bit):
    return (lax.axis_index("fsdp") >> bit) & 1


def swap(value, bit):
    count = lax.axis_size("fsdp")
    return lax.ppermute(value, "fsdp", [(i, i ^ (1 << bit)) for i in range(count)])


def pick(value, axis, index):
    return lax.dynamic_index_in_dim(value, index, axis, keepdims=False)


def rotations():
    bits = (lax.axis_size("fsdp") - 1).bit_length()
    if bits == 5:
        return ((1, 2, 3, 4), (2, 3, 4, 1), (3, 4, 1, 2))
    rest = tuple(range(1, bits))
    third = max(1, len(rest) // 3)
    return (rest, rest[third:] + rest[:third], rest[2 * third :] + rest[: 2 * third])


def tie(*values):
    return lax.optimization_barrier(values)


class Gathering:
    def __init__(self, shard, order):
        self.width = shard.shape[-1]
        self.order = tuple(reversed(order)) + (0,)
        self.held = shard
        self.have = []
        self.other = None

    def send(self):
        if len(self.have) < len(self.order):
            self.other = swap(self.held, self.order[len(self.have)])

    def step(self, value):
        self.join()
        if len(self.have) < len(self.order):
            self.held, value = tie(self.held, value)
        self.send()
        return value

    def join(self):
        if self.other is None:
            return
        bit = self.order[len(self.have)]
        place = sum(1 for item in self.have if item > bit)
        shape = self.held.shape[:place] + (2,) + self.held.shape[place:]
        own = lax.broadcasted_iota(jnp.int32, shape, place) == bit_value(bit)
        self.held = jnp.where(own, jnp.expand_dims(self.held, place), jnp.expand_dims(self.other, place))
        self.have.append(bit)
        self.other = None

    def finish(self, *widths):
        mine = bit_value(0)
        outs = []
        first = 0
        for width in widths:
            columns = slice(first, first + width)
            held, other = self.held[..., columns], self.other[..., columns]
            place = len(self.have)
            shape = held.shape[:place] + (2,) + held.shape[place:]
            own = lax.broadcasted_iota(jnp.int32, shape, place) == mine
            joined = jnp.where(own, jnp.expand_dims(held, place), jnp.expand_dims(other, place))
            outs.append(joined.reshape(-1, width))
            first = first + width
        return outs


class Scattering:
    def __init__(self, grad, order):
        self.order = (0,) + tuple(order)
        self.left = sorted(self.order, reverse=True)
        self.width = grad.shape[1]
        self.parts = [grad.astype(BF).reshape((2,) * len(self.order) + (-1, self.width))]
        self.done = 0

    def split(self):
        bit = self.order[self.done]
        axis = self.left.index(bit)
        mine = bit_value(bit)
        self.keep = sum(pick(item, axis, mine).astype(F32) for item in self.parts).astype(BF)
        self.left.remove(bit)
        return sum(pick(item, axis, 1 - mine).astype(F32) for item in self.parts).astype(BF)

    def send(self, away):
        self.parts = [self.keep, swap(away, self.order[self.done])]
        self.done = self.done + 1

    def total(self):
        return sum(item.astype(F32) for item in self.parts).reshape(-1, self.width)


def scatter_step(streams, *values):
    live = [item for item in streams if item.done < len(item.order)]
    away = [item.split() for item in live]
    tied = list(tie(*away, *values))
    for item, value in zip(live, tied):
        item.send(value)
    return tied[len(live) :]


def chip_groups():
    return [[i for i in range(lax.axis_size("fsdp")) if i % 2 == c] for c in range(2)]


def chip_sum(grad):
    return lax.psum_scatter(grad, "fsdp", scatter_dimension=0, axis_index_groups=chip_groups(), tiled=True)


def advance(streams, *values):
    for item in streams:
        item.join()
    live = [item for item in streams if len(item.have) < len(item.order)]
    held = tie(*[item.held for item in live], *values)
    for item, value in zip(live, held):
        item.held = value
        item.send()
    return held[len(live) :]


def body(
    tokens,
    lengths,
    cotangent,
    ln1_gain,
    ln1_bias,
    w_qkv,
    b_qv,
    w_out,
    b_out,
    ln2_gain,
    ln2_bias,
    w_up,
    b_up,
    w_down,
    b_down,
    ln3_gain,
    ln3_bias,
    w_learn,
    b_learn,
    w_map,
):
    micro, local, slots, _ = tokens.shape
    images = micro * local
    shard_rows = w_qkv.shape[0]
    devices = D // shard_rows
    vectors = (
        ln1_gain, ln1_bias, b_out, ln2_gain, ln2_bias, b_down, ln3_gain, ln3_bias, b_learn, b_qv, b_up,
    )
    lines = jnp.concatenate([item.reshape(-1, shard_rows).T for item in vectors], axis=1)
    line_count = lines.shape[1]
    small_count = line_count + w_map.shape[1]
    pad = (-small_count) % 128
    order_x, order_y, order_z = rotations()
    small = jnp.concatenate([lines, w_map, jnp.zeros((shard_rows, pad), BF)], axis=1)
    wide = gather(jnp.concatenate([w_up, w_out, w_learn], axis=1))
    w_down = gather(w_down)
    streams = [
        Gathering(w_qkv[:, D : 2 * D], order_y),
        Gathering(w_qkv[:, 2 * D :], order_z),
        Gathering(jnp.concatenate([w_qkv[:, :D], small], axis=1), order_x),
    ]
    for _ in range(len(streams[0].order)):
        advance(streams)
    (w_k,) = streams[0].finish(D)
    (w_v,) = streams[1].finish(D)
    w_q, spread = streams[2].finish(D, small.shape[1])
    w_qkv = jnp.concatenate([w_q, w_k, w_v], axis=1)
    spread = spread[:, :small_count]
    w_out = wide[:, 4 * D : 5 * D]
    w_learn = wide[:, 5 * D :]
    lines = spread[:, :line_count].T.astype(F32)
    named = []
    offset = 0
    for item in vectors:
        count = item.shape[0] // shard_rows
        part = lines[offset : offset + count]
        if count > 1:
            part = part.reshape(count, devices, shard_rows).transpose(1, 0, 2)
        named.append(part.reshape(1, -1))
        offset = offset + count
    (ln1_gain, ln1_bias, b_out, ln2_gain, ln2_bias, b_down, ln3_gain, ln3_bias, b_learn, b_qv, b_up) = named
    w_map = spread[:, offset:]
    lengths = lengths.reshape(images)
    row_total = images * slots
    source = tokens.reshape(row_total, D).astype(F32)
    hidden = layer_norm(source, ln1_gain, ln1_bias).astype(BF)
    qkv_bias = jnp.concatenate([b_qv[:, :D], jnp.zeros((1, D), F32), b_qv[:, D:]], axis=1)
    qkv = (mm(hidden, w_qkv, NN) + qkv_bias).astype(BF)
    filled = ()
    for image in range(images):
        filled = attention_forward(image, qkv, lengths, filled)
    attended, lse = filled
    middle = source + mm(attended, w_out, NN) + b_out
    normed = layer_norm(middle, ln2_gain, ln2_bias).astype(BF)
    up_act, up_slope = gelu_matmul(normed, [(wide, 0, 4 * D)], b_up)
    output = middle + mm(up_act, w_down, NN) + b_down
    learn_in = layer_norm(output, ln3_gain, ln3_bias).astype(BF)
    learn_act, learn_slope = gelu_matmul(learn_in, [(wide, 5 * D, D)], b_learn)
    logits = mm(learn_act, w_map, NN)
    slot_valid = lax.broadcasted_iota(jnp.int32, (images, slots, 1), 1) < lengths[:, None, None]
    pool_share = (slot_valid.astype(F32) / lengths[:, None, None].astype(F32)).reshape(row_total, 1)
    squashed = jax.nn.sigmoid(logits)
    pool_maps = (squashed * pool_share).reshape(images, slots, -1)
    by_image = output.reshape(images, slots, D)
    pooled = jnp.einsum("bsm,bsd->bmd", pool_maps, by_image, precision=lax.Precision.HIGHEST)
    pool_grad = cotangent.reshape(images, -1, D)
    d_maps = jnp.einsum("bsd,bmd->bsm", by_image, pool_grad, precision=lax.Precision.HIGHEST)
    d_maps = d_maps.reshape(row_total, -1)
    d_output = jnp.einsum("bsm,bmd->bsd", pool_maps, pool_grad, precision=lax.Precision.HIGHEST)
    d_output = d_output.reshape(row_total, D)
    d_logits = (d_maps * pool_share * squashed * (1.0 - squashed)).astype(BF)
    g_map = mm(learn_act, d_logits, TN)
    d_learn = (learn_slope.astype(F32) * mm(d_logits, w_map, NT)).astype(BF)
    g_blearn = jnp.sum(d_learn.astype(F32), axis=0)
    d_norm3, g_ln3, h_ln3 = norm_back(output, ln3_gain, mm(d_learn, w_learn, NT))
    d_output = d_output + d_norm3
    d_mlp = d_output.astype(BF)
    g_bdown = jnp.sum(d_mlp.astype(F32), axis=0)
    mine = bit_value(0)

    def core_parts(grad):
        blocks = grad.astype(BF).reshape(devices // 2, 2, -1, grad.shape[1])
        return pick(blocks, 1, mine), pick(blocks, 1, 1 - mine)

    def add(left, right):
        return (left.astype(F32) + right.astype(F32)).astype(BF)

    keep, away = core_parts(mm(up_act, d_mlp, TN))
    keep, away, d_learn = tie(keep, away, d_learn)
    other = swap(away, 0)
    g_wlearn = mm(learn_in, d_learn, TN).astype(BF)
    other, keep, g_wlearn, d_mlp = tie(other, keep, g_wlearn, d_mlp)
    g_down = add(keep, other)
    g_down, d_mlp = tie(g_down, d_mlp)
    g_wdown = chip_sum(g_down.reshape(-1, D)).astype(F32)
    d_up, g_bup = slope_matmul(d_mlp, w_down, up_slope)
    up_keep, up_away = core_parts(mm(normed, d_up, TN))
    up_keep, up_away, d_up = tie(up_keep, up_away, d_up)
    up_other = swap(up_away, 0)
    d_normed = back_product([d_up], wide)
    d_norm2, g_ln2, h_ln2 = norm_back(middle, ln2_gain, d_normed)
    d_middle = d_output + d_norm2
    d_branch = d_middle.astype(BF)
    up_other, d_branch = tie(up_other, d_branch)
    g_up = add(up_keep, up_other)
    g_up, d_branch = tie(g_up, d_branch)
    g_wup = chip_sum(g_up.reshape(-1, g_up.shape[-1])).astype(F32)
    g_bout = jnp.sum(d_branch.astype(F32), axis=0)
    out_stream = Scattering(jnp.concatenate([mm(attended, d_branch, TN).astype(BF), g_wlearn], axis=1), order_y)
    d_attended = mm(d_branch, w_out, NT).astype(BF)
    (d_attended,) = scatter_step([out_stream], d_attended)
    filled = ()
    for image in range(images):
        filled = attention_backward(image, qkv, attended, d_attended, lse, lengths, filled)
        filled = scatter_step([out_stream], *filled)
    late = []
    parts = list(filled)
    for n, order in enumerate((order_x, order_y, order_z)):
        stream = Scattering(mm(hidden, parts[n], TN), order)
        parts = scatter_step([stream], *parts)
        late.append(stream)
    d_hidden = back_product(parts, w_qkv)
    g_bqv = jnp.concatenate([jnp.sum(item.astype(F32), axis=0) for item in (parts[0], parts[2])])
    (d_hidden,) = scatter_step(late, d_hidden)
    d_norm1, g_ln1, h_ln1 = norm_back(source, ln1_gain, d_hidden)
    grads = (g_ln1, h_ln1, g_bout, g_ln2, h_ln2, g_bdown, g_ln3, h_ln3, g_blearn, g_bqv, g_bup)
    lines = jnp.concatenate(
        [item.reshape(devices, -1, shard_rows).transpose(1, 0, 2).reshape(-1, D) for item in grads], axis=0
    )
    spread = jnp.concatenate([lines.T, g_map, jnp.zeros((D, pad), F32)], axis=1)
    (spread,) = scatter_step(late, spread)
    small = Scattering(spread, order_z)
    d_image = (d_middle + d_norm1).reshape(tokens.shape)
    (d_image,) = scatter_step([small], d_image)
    for _ in range(len(small.order)):
        (d_image,) = scatter_step(late + [small], d_image)
    for _ in range(len(small.order)):
        (d_image,) = scatter_step([out_stream], d_image)
    g_wqkv = jnp.concatenate([item.total() for item in late], axis=1)
    small = small.total()
    joint = out_stream.total()
    g_wout = joint[:, :D]
    g_wlearn = joint[:, D:]
    outs = []
    offset = 0
    for item in vectors:
        count = item.shape[0] // shard_rows
        outs.append(small[:, offset : offset + count].T.reshape(-1))
        offset = offset + count
    (g_ln1, h_ln1, g_bout, g_ln2, h_ln2, g_bdown, g_ln3, h_ln3, g_blearn, g_bqv, g_bup) = outs
    g_map = small[:, offset:small_count]
    pooled = pooled.reshape(cotangent.shape)
    return (
        pooled, d_image, g_ln1, h_ln1, g_wqkv, g_bqv, g_wout, g_bout, g_ln2, h_ln2,
        g_wup, g_bup, g_wdown, g_bdown, g_ln3, h_ln3, g_wlearn, g_blearn, g_map,
    )


def solution(mesh):
    rows = P("fsdp", None)
    line = P("fsdp")
    batch = P(None, "fsdp", None, None)
    params = (line, line, rows, line, rows, line, line, line, rows, line, rows, line, line, line, rows, line, rows)
    return jax.shard_map(
        body,
        mesh=mesh,
        in_specs=(batch, P(None, "fsdp"), batch) + params,
        out_specs=(batch, batch) + params,
        check_vma=False,
    )
```

```python
import functools

import jax
import jax.numpy as jnp
from jax import lax
from jax.experimental import pallas as pl
from jax.experimental.pallas import tpu as pltpu
from jax.sharding import PartitionSpec as P

D = 1024
HEADS = 16
HD = 64
PAIR = 2 * HD
EPSILON = 1e-06
SCALE = 0.125
LOG2E = 1.4426950408889634
SHORT_ROWS = 256
PAIRS = 2
BF = jnp.bfloat16
F32 = jnp.float32

NN = (((1,), (0,)), ((), ()))
NT = (((1,), (1,)), ((), ()))
TN = (((0,), (0,)), ((), ()))


def mm(left, right, dims):
    return lax.dot_general(left, right, dims, preferred_element_type=F32)


def layer_norm_parts(values):
    row_mean = jnp.mean(values, axis=-1, keepdims=True)
    centered = values - row_mean
    variance = jnp.mean(centered * centered, axis=-1, keepdims=True)
    rstd = lax.rsqrt(variance + EPSILON)
    return centered * rstd, rstd


def layer_norm(values, gain, shift):
    return layer_norm_parts(values)[0] * gain + shift


def norm_back(values, gain, incoming):
    normed, rstd = layer_norm_parts(values)
    scaled = incoming * gain
    grad = rstd * (
        scaled
        - jnp.mean(scaled, axis=-1, keepdims=True)
        - normed * jnp.mean(scaled * normed, axis=-1, keepdims=True)
    )
    return grad, jnp.sum(incoming * normed, axis=0), jnp.sum(incoming, axis=0)


ERFCX = (
    0.18636609783492827,
    0.1828374067871815,
    0.2019228837403338,
    0.045013532984771946,
    0.4125364399329413,
    -0.3554335531070661,
    0.46268519224041466,
    -0.13592808196895617,
)
ERFCX_SCALE = 0.33


def gelu_with_slope(values):
    near = 1.0 / (1.0 + jnp.abs(values) * (ERFCX_SCALE * 0.5**0.5))
    series = 0.5 * ERFCX[-1] * near + 0.5 * ERFCX[-2]
    for item in ERFCX[-3::-1]:
        series = series * near + 0.5 * item
    bell = jnp.exp2((values * values) * (-0.5 * LOG2E))
    tail = (bell * near) * series
    half = jnp.where(values < 0, tail, 1.0 - tail)
    return values * half, half + values * (bell * 0.3989422804014327)


def gelu_matmul_kernel(chunk, tiles, x_ref, b_ref, *refs):
    w_refs = refs[: len(tiles)]
    act_ref, slope_ref = refs[len(tiles) :]
    step = pl.program_id(0)
    first = 0
    for w_ref, count in zip(w_refs, tiles):

        @pl.when((step >= first) & (step < first + count))
        def _(w_ref=w_ref):
            for start in range(0, x_ref.shape[0], chunk):
                rows = pl.ds(start, chunk)
                act, slope = gelu_with_slope(mm(x_ref[rows], w_ref[...], NN) + b_ref[...])
                act_ref[rows] = act.astype(BF)
                slope_ref[rows] = slope.astype(BF)

        first = first + count


def slope_matmul_kernel(chunk, x_ref, w_ref, slope_ref, out_ref, sum_ref):
    total = jnp.zeros(sum_ref.shape, F32)
    for start in range(0, x_ref.shape[0], chunk):
        rows = pl.ds(start, chunk)
        out = (mm(x_ref[rows], w_ref[...], NT) * slope_ref[rows].astype(F32)).astype(BF)
        out_ref[rows] = out
        total = total + jnp.sum(out.astype(F32), axis=0, keepdims=True)
    sum_ref[...] = total


def light():
    return pl.CostEstimate(flops=1024, bytes_accessed=1024, transcendentals=0)


def gelu_matmul(x, pieces, bias):
    rows, inner = x.shape
    tile = 512
    width = bias.shape[1]
    tiles = [item[2] // tile for item in pieces]
    specs = []
    before = 0
    for (_, first, _), count in zip(pieces, tiles):

        def place(j, first=first, before=before, count=count):
            return 0, first // tile + jnp.clip(j - before, 0, count - 1)

        specs.append(pl.BlockSpec((inner, tile), place))
        before = before + count
    out = pl.BlockSpec((rows, tile), lambda j: (0, j))
    return pl.pallas_call(
        functools.partial(gelu_matmul_kernel, rows // 4, tiles),
        out_shape=(jax.ShapeDtypeStruct((rows, width), BF),) * 2,
        grid=(width // tile,),
        in_specs=[pl.BlockSpec((rows, inner), lambda j: (0, 0)), pl.BlockSpec((1, tile), lambda j: (0, j))] + specs,
        out_specs=(out, out),
        cost_estimate=light(),
        name="gelu_matmul",
    )(x, bias, *[item[0] for item in pieces])


def back_product_kernel(count, *refs):
    total = mm(refs[0][...], refs[count][...], NT)
    for i in range(1, count):
        total = total + mm(refs[i][...], refs[count + i][...], NT)
    refs[-1][...] = total


def back_product(pieces, weights):
    count = len(pieces)
    rows, width = pieces[0].shape
    height = weights[0].shape[0]
    tile = 512
    whole = pl.BlockSpec((rows, width), lambda j: (0, 0))
    part = pl.BlockSpec((tile, width), lambda j: (j, 0))
    return pl.pallas_call(
        functools.partial(back_product_kernel, count),
        out_shape=jax.ShapeDtypeStruct((rows, height), F32),
        grid=(height // tile,),
        in_specs=[whole] * count + [part] * count,
        out_specs=pl.BlockSpec((rows, tile), lambda j: (0, j)),
        cost_estimate=light(),
        name="back_product",
    )(*pieces, *weights)


def slope_matmul(x, w, slope):
    rows, inner = x.shape
    width = w.shape[0]
    tile = 1024
    block = pl.BlockSpec((rows, tile), lambda j: (0, j))
    return pl.pallas_call(
        functools.partial(slope_matmul_kernel, rows // 4),
        out_shape=(jax.ShapeDtypeStruct((rows, width), BF), jax.ShapeDtypeStruct((1, width), F32)),
        grid=(width // tile,),
        in_specs=[
            pl.BlockSpec((rows, inner), lambda j: (0, 0)),
            pl.BlockSpec((tile, inner), lambda j: (j, 0)),
            block,
        ],
        out_specs=(block, pl.BlockSpec((1, tile), lambda j: (0, j))),
        cost_estimate=light(),
        name="slope_matmul",
    )(x, w, slope)


def head_lanes(shape, head):
    return (lax.broadcasted_iota(jnp.int32, shape, 1) // HD) == head


def key_mask(scores, length):
    return jnp.where(lax.broadcasted_iota(jnp.int32, scores.shape, 0) < length, scores, -1e30)


def attention_forward_kernel(slots, image, len_ref, q_ref, k_ref, v_ref, o_ref, lse_ref):
    length = len_ref[image]

    def attend(rows, masked):
        for pair in range(PAIRS):
            lanes = pl.ds(pair * PAIR, PAIR)
            q = q_ref[:rows, lanes]
            k = k_ref[:rows, lanes]
            v_t = v_ref[:rows, lanes].T
            outs = []
            for head in range(2):
                q_one = jnp.where(head_lanes(q.shape, head), q, jnp.zeros_like(q))
                scores = mm(k, q_one, NT)
                if masked:
                    scores = key_mask(scores, length)
                top = jnp.max(scores, axis=0, keepdims=True)
                probs = jnp.exp2((scores - top) * (SCALE * LOG2E))
                total = jnp.sum(probs, axis=0, keepdims=True)
                out = mm(v_t[head * HD : (head + 1) * HD], probs.astype(BF), NN)
                outs.append(out * (1.0 / total))
                lse_ref[0, pair * 2 + head : pair * 2 + head + 1, :rows] = top * (
                    SCALE * LOG2E
                ) + jnp.log2(total)
            o_ref[:rows, lanes] = jnp.concatenate(outs, 0).astype(BF).T

    @pl.when(length > SHORT_ROWS)
    def _():
        attend(slots, False)

    @pl.when(length <= SHORT_ROWS)
    def _():
        o_ref[...] = jnp.zeros_like(o_ref)
        lse_ref[...] = jnp.zeros_like(lse_ref)
        attend(SHORT_ROWS, True)


def attention_backward_kernel(
    slots, image, len_ref, q_ref, k_ref, v_ref, o_ref, do_ref, lse_ref, dq_ref, dk_ref, dv_ref
):
    length = len_ref[image]

    def attend(rows, masked):
        for pair in range(PAIRS):
            lanes = pl.ds(pair * PAIR, PAIR)
            q = q_ref[:rows, lanes]
            k = k_ref[:rows, lanes]
            v = v_ref[:rows, lanes]
            do = do_ref[:rows, lanes]
            weighted = o_ref[:rows, lanes].astype(F32) * do.astype(F32)
            k_t = k.T
            zero = jnp.zeros_like(q)
            dqs = []
            dks = []
            dvs = []
            for head in range(2):
                own = head_lanes(q.shape, head)
                ones = jnp.where(head_lanes((8, PAIR), head), 1.0, 0.0)
                row_dot = lax.dot_general(
                    ones, weighted, NT, precision=lax.Precision.HIGHEST, preferred_element_type=F32
                )[0:1]
                scores = mm(k, jnp.where(own, q, zero), NT)
                if masked:
                    scores = key_mask(scores, length)
                lse = lse_ref[0, pair * 2 + head : pair * 2 + head + 1, :rows]
                probs = jnp.exp2(scores * (SCALE * LOG2E) - lse)
                d_probs = mm(v, jnp.where(own, do, zero), NT)
                d_scores = (probs * (d_probs - row_dot)).astype(BF)
                dvs.append(mm(probs.astype(BF), do, NN))
                dks.append(mm(d_scores, q, NN))
                dqs.append(mm(k_t[head * HD : (head + 1) * HD], d_scores, NN))
            low = head_lanes(dks[0].shape, 0)
            dv_ref[:rows, lanes] = jnp.where(low, dvs[0], dvs[1]).astype(BF)
            dk_ref[:rows, lanes] = (jnp.where(low, dks[0], dks[1]) * SCALE).astype(BF)
            dq_ref[:rows, lanes] = (jnp.concatenate(dqs, 0) * SCALE).astype(BF).T

    @pl.when(length > SHORT_ROWS)
    def _():
        attend(slots, False)

    @pl.when(length <= SHORT_ROWS)
    def _():
        for ref in (dq_ref, dk_ref, dv_ref):
            ref[...] = jnp.zeros_like(ref)
        attend(SHORT_ROWS, True)


def head_blocks(slots, image, part=0):
    first = part * (HEADS // (2 * PAIRS))
    return pl.BlockSpec((slots, PAIRS * PAIR), lambda h, lens: (image, first + h))


def lse_blocks(slots, image):
    steps = HEADS // (2 * PAIRS)
    return pl.BlockSpec((1, 2 * PAIRS, slots), lambda h, lens: (image * steps + h, 0, 0))


def held_in_place(kernel, count):
    def whole(len_ref, *refs):
        return kernel(len_ref, *refs[count:])

    return whole


def attention_forward(image, qkv, lengths, filled):
    images = lengths.shape[0]
    slots = qkv.shape[0] // images
    steps = HEADS // (2 * PAIRS)
    block = head_blocks(slots, image)
    outs = (block, lse_blocks(slots, image))
    kernel = functools.partial(attention_forward_kernel, slots, image)
    anywhere = [pl.BlockSpec(memory_space=pl.ANY)] * len(filled)
    return pl.pallas_call(
        held_in_place(kernel, len(filled)),
        out_shape=(
            jax.ShapeDtypeStruct((images * slots, D), BF),
            jax.ShapeDtypeStruct((images * steps, 2 * PAIRS, slots), F32),
        ),
        grid_spec=pltpu.PrefetchScalarGridSpec(
            num_scalar_prefetch=1,
            grid=(steps,),
            in_specs=anywhere + [head_blocks(slots, image, part) for part in range(3)],
            out_specs=outs,
        ),
        input_output_aliases={1 + i: i for i in range(len(filled))},
        cost_estimate=light(),
        name="attention_forward",
    )(lengths, *filled, qkv, qkv, qkv)


def attention_backward(image, qkv, attended, d_attended, lse, lengths, filled):
    images = lengths.shape[0]
    slots = qkv.shape[0] // images
    steps = HEADS // (2 * PAIRS)
    block = head_blocks(slots, image)
    kernel = functools.partial(attention_backward_kernel, slots, image)
    anywhere = [pl.BlockSpec(memory_space=pl.ANY)] * len(filled)
    return pl.pallas_call(
        held_in_place(kernel, len(filled)),
        out_shape=tuple(jax.ShapeDtypeStruct((images * slots, D), BF) for _ in range(3)),
        grid_spec=pltpu.PrefetchScalarGridSpec(
            num_scalar_prefetch=1,
            grid=(steps,),
            in_specs=anywhere
            + [head_blocks(slots, image, part) for part in range(3)]
            + [block] * 2
            + [lse_blocks(slots, image)],
            out_specs=(block, block, block),
        ),
        input_output_aliases={1 + i: i for i in range(len(filled))},
        cost_estimate=light(),
        name="attention_backward",
    )(lengths, *filled, qkv, qkv, qkv, attended, d_attended, lse)


def gather(shard):
    return lax.all_gather(shard, "fsdp", axis=0, tiled=True)


def scatter_sum(grad):
    return lax.psum_scatter(grad.astype(BF), "fsdp", scatter_dimension=0, tiled=True).astype(F32)


def bit_value(bit):
    return (lax.axis_index("fsdp") >> bit) & 1


def swap(value, bit):
    count = lax.axis_size("fsdp")
    return lax.ppermute(value, "fsdp", [(i, i ^ (1 << bit)) for i in range(count)])


def pick(value, axis, index):
    return lax.dynamic_index_in_dim(value, index, axis, keepdims=False)


def rotations():
    bits = (lax.axis_size("fsdp") - 1).bit_length()
    if bits == 5:
        return ((1, 2, 3, 4), (2, 3, 4, 1), (3, 4, 1, 2))
    rest = tuple(range(1, bits))
    third = max(1, len(rest) // 3)
    return (rest, rest[third:] + rest[:third], rest[2 * third :] + rest[: 2 * third])


def tie(*values):
    return lax.optimization_barrier(values)


class Gathering:
    def __init__(self, shard, order):
        self.width = shard.shape[-1]
        self.order = tuple(reversed(order)) + (0,)
        self.held = shard
        self.have = []
        self.other = None

    def send(self):
        if len(self.have) < len(self.order):
            self.other = swap(self.held, self.order[len(self.have)])

    def step(self, value):
        self.join()
        if len(self.have) < len(self.order):
            self.held, value = tie(self.held, value)
        self.send()
        return value

    def join(self):
        if self.other is None:
            return
        bit = self.order[len(self.have)]
        place = sum(1 for item in self.have if item > bit)
        shape = self.held.shape[:place] + (2,) + self.held.shape[place:]
        own = lax.broadcasted_iota(jnp.int32, shape, place) == bit_value(bit)
        self.held = jnp.where(own, jnp.expand_dims(self.held, place), jnp.expand_dims(self.other, place))
        self.have.append(bit)
        self.other = None

    def finish(self, *widths):
        mine = bit_value(0)
        outs = []
        first = 0
        for width in widths:
            columns = slice(first, first + width)
            held, other = self.held[..., columns], self.other[..., columns]
            place = len(self.have)
            shape = held.shape[:place] + (2,) + held.shape[place:]
            own = lax.broadcasted_iota(jnp.int32, shape, place) == mine
            joined = jnp.where(own, jnp.expand_dims(held, place), jnp.expand_dims(other, place))
            outs.append(joined.reshape(-1, width))
            first = first + width
        return outs


class Scattering:
    def __init__(self, grad, order):
        self.order = (0,) + tuple(order)
        self.left = sorted(self.order, reverse=True)
        self.width = grad.shape[1]
        self.parts = [grad.astype(BF).reshape((2,) * len(self.order) + (-1, self.width))]
        self.done = 0

    def split(self):
        bit = self.order[self.done]
        axis = self.left.index(bit)
        mine = bit_value(bit)
        self.keep = sum(pick(item, axis, mine).astype(F32) for item in self.parts).astype(BF)
        self.left.remove(bit)
        return sum(pick(item, axis, 1 - mine).astype(F32) for item in self.parts).astype(BF)

    def send(self, away):
        self.parts = [self.keep, swap(away, self.order[self.done])]
        self.done = self.done + 1

    def total(self):
        return sum(item.astype(F32) for item in self.parts).reshape(-1, self.width)


def scatter_step(streams, *values):
    live = [item for item in streams if item.done < len(item.order)]
    away = [item.split() for item in live]
    tied = list(tie(*away, *values))
    for item, value in zip(live, tied):
        item.send(value)
    return tied[len(live) :]


def chip_groups():
    return [[i for i in range(lax.axis_size("fsdp")) if i % 2 == c] for c in range(2)]


def chip_sum(grad):
    return lax.psum_scatter(grad, "fsdp", scatter_dimension=0, axis_index_groups=chip_groups(), tiled=True)


def advance(streams, *values):
    for item in streams:
        item.join()
    live = [item for item in streams if len(item.have) < len(item.order)]
    held = tie(*[item.held for item in live], *values)
    for item, value in zip(live, held):
        item.held = value
        item.send()
    return held[len(live) :]


def body(
    tokens,
    lengths,
    cotangent,
    ln1_gain,
    ln1_bias,
    w_qkv,
    b_qv,
    w_out,
    b_out,
    ln2_gain,
    ln2_bias,
    w_up,
    b_up,
    w_down,
    b_down,
    ln3_gain,
    ln3_bias,
    w_learn,
    b_learn,
    w_map,
):
    micro, local, slots, _ = tokens.shape
    images = micro * local
    shard_rows = w_qkv.shape[0]
    devices = D // shard_rows
    vectors = (
        ln1_gain, ln1_bias, b_out, ln2_gain, ln2_bias, b_down, ln3_gain, ln3_bias, b_learn, b_qv, b_up,
    )
    lines = jnp.concatenate([item.reshape(-1, shard_rows).T for item in vectors], axis=1)
    line_count = lines.shape[1]
    small_count = line_count + w_map.shape[1]
    pad = (-small_count) % 128
    order_x, order_y, order_z = rotations()
    small = jnp.concatenate([lines, w_map, jnp.zeros((shard_rows, pad), BF)], axis=1)
    wide = gather(jnp.concatenate([w_up, w_out, w_learn], axis=1))
    w_down = gather(w_down)
    streams = [
        Gathering(w_qkv[:, D : 2 * D], order_y),
        Gathering(w_qkv[:, 2 * D :], order_z),
        Gathering(jnp.concatenate([w_qkv[:, :D], small], axis=1), order_x),
    ]
    for _ in range(len(streams[0].order)):
        advance(streams)
    (w_k,) = streams[0].finish(D)
    (w_v,) = streams[1].finish(D)
    w_q, spread = streams[2].finish(D, small.shape[1])
    w_qkv = jnp.concatenate([w_q, w_k, w_v], axis=1)
    spread = spread[:, :small_count]
    w_out = wide[:, 4 * D : 5 * D]
    w_learn = wide[:, 5 * D :]
    lines = spread[:, :line_count].T.astype(F32)
    named = []
    offset = 0
    for item in vectors:
        count = item.shape[0] // shard_rows
        part = lines[offset : offset + count]
        if count > 1:
            part = part.reshape(count, devices, shard_rows).transpose(1, 0, 2)
        named.append(part.reshape(1, -1))
        offset = offset + count
    (ln1_gain, ln1_bias, b_out, ln2_gain, ln2_bias, b_down, ln3_gain, ln3_bias, b_learn, b_qv, b_up) = named
    w_map = spread[:, offset:]
    lengths = lengths.reshape(images)
    row_total = images * slots
    source = tokens.reshape(row_total, D).astype(F32)
    hidden = layer_norm(source, ln1_gain, ln1_bias).astype(BF)
    qkv_bias = jnp.concatenate([b_qv[:, :D], jnp.zeros((1, D), F32), b_qv[:, D:]], axis=1)
    qkv = (mm(hidden, w_qkv, NN) + qkv_bias).astype(BF)
    filled = ()
    for image in range(images):
        filled = attention_forward(image, qkv, lengths, filled)
    attended, lse = filled
    middle = source + mm(attended, w_out, NN) + b_out
    normed = layer_norm(middle, ln2_gain, ln2_bias).astype(BF)
    up_act, up_slope = gelu_matmul(normed, [(wide, 0, 4 * D)], b_up)
    output = middle + mm(up_act, w_down, NN) + b_down
    learn_in = layer_norm(output, ln3_gain, ln3_bias).astype(BF)
    learn_act, learn_slope = gelu_matmul(learn_in, [(wide, 5 * D, D)], b_learn)
    logits = mm(learn_act, w_map, NN)
    slot_valid = lax.broadcasted_iota(jnp.int32, (images, slots, 1), 1) < lengths[:, None, None]
    pool_share = (slot_valid.astype(F32) / lengths[:, None, None].astype(F32)).reshape(row_total, 1)
    squashed = jax.nn.sigmoid(logits)
    pool_maps = (squashed * pool_share).reshape(images, slots, -1)
    by_image = output.reshape(images, slots, D)
    pooled = jnp.einsum("bsm,bsd->bmd", pool_maps, by_image, precision=lax.Precision.HIGHEST)
    pool_grad = cotangent.reshape(images, -1, D)
    d_maps = jnp.einsum("bsd,bmd->bsm", by_image, pool_grad, precision=lax.Precision.HIGHEST)
    d_maps = d_maps.reshape(row_total, -1)
    d_output = jnp.einsum("bsm,bmd->bsd", pool_maps, pool_grad, precision=lax.Precision.HIGHEST)
    d_output = d_output.reshape(row_total, D)
    d_logits = (d_maps * pool_share * squashed * (1.0 - squashed)).astype(BF)
    g_map = mm(learn_act, d_logits, TN)
    d_learn = (learn_slope.astype(F32) * mm(d_logits, w_map, NT)).astype(BF)
    g_blearn = jnp.sum(d_learn.astype(F32), axis=0)
    d_norm3, g_ln3, h_ln3 = norm_back(output, ln3_gain, mm(d_learn, w_learn, NT))
    d_output = d_output + d_norm3
    d_mlp = d_output.astype(BF)
    g_bdown = jnp.sum(d_mlp.astype(F32), axis=0)
    mine = bit_value(0)

    def core_parts(grad):
        blocks = grad.astype(BF).reshape(devices // 2, 2, -1, grad.shape[1])
        return pick(blocks, 1, mine), pick(blocks, 1, 1 - mine)

    def add(left, right):
        return (left.astype(F32) + right.astype(F32)).astype(BF)

    keep, away = core_parts(mm(up_act, d_mlp, TN))
    keep, away, d_learn = tie(keep, away, d_learn)
    other = swap(away, 0)
    g_wlearn = mm(learn_in, d_learn, TN).astype(BF)
    other, keep, g_wlearn, d_mlp = tie(other, keep, g_wlearn, d_mlp)
    g_down = add(keep, other)
    g_down, d_mlp = tie(g_down, d_mlp)
    g_wdown = chip_sum(g_down.reshape(-1, D)).astype(F32)
    d_up, g_bup = slope_matmul(d_mlp, w_down, up_slope)
    up_keep, up_away = core_parts(mm(normed, d_up, TN))
    up_keep, up_away, d_up = tie(up_keep, up_away, d_up)
    up_other = swap(up_away, 0)
    d_normed = back_product([d_up], [wide])
    d_norm2, g_ln2, h_ln2 = norm_back(middle, ln2_gain, d_normed)
    d_middle = d_output + d_norm2
    d_branch = d_middle.astype(BF)
    g_bout = jnp.sum(d_branch.astype(F32), axis=0)
    out_stream = Scattering(jnp.concatenate([mm(attended, d_branch, TN).astype(BF), g_wlearn], axis=1), order_y)
    d_attended = mm(d_branch, w_out, NT).astype(BF)
    (d_attended,) = scatter_step([out_stream], d_attended)
    filled = attention_backward(0, qkv, attended, d_attended, lse, lengths, ())
    up_other, up_keep, *filled = scatter_step([out_stream], up_other, up_keep, *filled)
    g_up = add(up_keep, up_other)
    g_up, *filled = tie(g_up, *filled)
    g_wup = chip_sum(g_up.reshape(-1, g_up.shape[-1])).astype(F32)
    for image in range(1, images):
        filled = attention_backward(image, qkv, attended, d_attended, lse, lengths, filled)
    filled = scatter_step([out_stream], *filled)
    late = []
    parts = list(filled)
    for n, order in enumerate((order_x, order_y, order_z)):
        stream = Scattering(mm(hidden, parts[n], TN), order)
        parts = scatter_step([stream], *parts)
        late.append(stream)
    g_bqv = jnp.concatenate([jnp.sum(item.astype(F32), axis=0) for item in (parts[0], parts[2])])
    g_bqv, *parts = scatter_step(late, g_bqv, *parts)
    d_hidden = back_product(parts, [w_q, w_k, w_v])
    d_norm1, g_ln1, h_ln1 = norm_back(source, ln1_gain, d_hidden)
    grads = (g_ln1, h_ln1, g_bout, g_ln2, h_ln2, g_bdown, g_ln3, h_ln3, g_blearn, g_bqv, g_bup)
    lines = jnp.concatenate(
        [item.reshape(devices, -1, shard_rows).transpose(1, 0, 2).reshape(-1, D) for item in grads], axis=0
    )
    spread = jnp.concatenate([lines.T, g_map, jnp.zeros((D, pad), F32)], axis=1)
    small = Scattering(spread, order_z)
    (pooled,) = scatter_step([small], pooled)
    d_image = (d_middle + d_norm1).reshape(tokens.shape)
    for _ in range(len(small.order)):
        (d_image,) = scatter_step(late + [out_stream], d_image)
        scatter_step([small])
    g_wqkv = jnp.concatenate([item.total() for item in late], axis=1)
    small = small.total()
    joint = out_stream.total()
    g_wout = joint[:, :D]
    g_wlearn = joint[:, D:]
    outs = []
    offset = 0
    for item in vectors:
        count = item.shape[0] // shard_rows
        outs.append(small[:, offset : offset + count].T.reshape(-1))
        offset = offset + count
    (g_ln1, h_ln1, g_bout, g_ln2, h_ln2, g_bdown, g_ln3, h_ln3, g_blearn, g_bqv, g_bup) = outs
    g_map = small[:, offset:small_count]
    pooled = pooled.reshape(cotangent.shape)
    return (
        pooled, d_image, g_ln1, h_ln1, g_wqkv, g_bqv, g_wout, g_bout, g_ln2, h_ln2,
        g_wup, g_bup, g_wdown, g_bdown, g_ln3, h_ln3, g_wlearn, g_blearn, g_map,
    )


def solution(mesh):
    rows = P("fsdp", None)
    line = P("fsdp")
    batch = P(None, "fsdp", None, None)
    params = (line, line, rows, line, rows, line, line, line, rows, line, rows, line, line, line, rows, line, rows)
    return jax.shard_map(
        body,
        mesh=mesh,
        in_specs=(batch, P(None, "fsdp"), batch) + params,
        out_specs=(batch, batch) + params,
        check_vma=False,
    )
```

```python
import functools

import jax
import jax.numpy as jnp
from jax import lax
from jax.experimental import pallas as pl
from jax.experimental.pallas import tpu as pltpu
from jax.sharding import PartitionSpec as P

D = 1024
HEADS = 16
HD = 64
PAIR = 2 * HD
EPSILON = 1e-06
SCALE = 0.125
LOG2E = 1.4426950408889634
SHORT_ROWS = 256
PAIRS = 2
BF = jnp.bfloat16
F32 = jnp.float32

NN = (((1,), (0,)), ((), ()))
NT = (((1,), (1,)), ((), ()))
TN = (((0,), (0,)), ((), ()))


def mm(left, right, dims):
    return lax.dot_general(left, right, dims, preferred_element_type=F32)


def layer_norm_parts(values):
    row_mean = jnp.mean(values, axis=-1, keepdims=True)
    centered = values - row_mean
    variance = jnp.mean(centered * centered, axis=-1, keepdims=True)
    rstd = lax.rsqrt(variance + EPSILON)
    return centered * rstd, rstd


def layer_norm(values, gain, shift):
    return layer_norm_parts(values)[0] * gain + shift


def norm_back(values, gain, incoming):
    normed, rstd = layer_norm_parts(values)
    scaled = incoming * gain
    grad = rstd * (
        scaled
        - jnp.mean(scaled, axis=-1, keepdims=True)
        - normed * jnp.mean(scaled * normed, axis=-1, keepdims=True)
    )
    return grad, jnp.sum(incoming * normed, axis=0), jnp.sum(incoming, axis=0)


ERFCX = (
    0.18636609783492827,
    0.1828374067871815,
    0.2019228837403338,
    0.045013532984771946,
    0.4125364399329413,
    -0.3554335531070661,
    0.46268519224041466,
    -0.13592808196895617,
)
ERFCX_SCALE = 0.33


def gelu_with_slope(values):
    near = 1.0 / (1.0 + jnp.abs(values) * (ERFCX_SCALE * 0.5**0.5))
    series = 0.5 * ERFCX[-1] * near + 0.5 * ERFCX[-2]
    for item in ERFCX[-3::-1]:
        series = series * near + 0.5 * item
    bell = jnp.exp2((values * values) * (-0.5 * LOG2E))
    tail = (bell * near) * series
    half = jnp.where(values < 0, tail, 1.0 - tail)
    return values * half, half + values * (bell * 0.3989422804014327)


def gelu_matmul_kernel(chunk, tiles, x_ref, b_ref, *refs):
    w_refs = refs[: len(tiles)]
    act_ref, slope_ref = refs[len(tiles) :]
    step = pl.program_id(0)
    first = 0
    for w_ref, count in zip(w_refs, tiles):

        @pl.when((step >= first) & (step < first + count))
        def _(w_ref=w_ref):
            for start in range(0, x_ref.shape[0], chunk):
                rows = pl.ds(start, chunk)
                act, slope = gelu_with_slope(mm(x_ref[rows], w_ref[...], NN) + b_ref[...])
                act_ref[rows] = act.astype(BF)
                slope_ref[rows] = slope.astype(BF)

        first = first + count


def slope_matmul_kernel(chunk, x_ref, w_ref, slope_ref, out_ref, sum_ref):
    total = jnp.zeros(sum_ref.shape, F32)
    for start in range(0, x_ref.shape[0], chunk):
        rows = pl.ds(start, chunk)
        out = (mm(x_ref[rows], w_ref[...], NT) * slope_ref[rows].astype(F32)).astype(BF)
        out_ref[rows] = out
        total = total + jnp.sum(out.astype(F32), axis=0, keepdims=True)
    sum_ref[...] = total


def light():
    return pl.CostEstimate(flops=1024, bytes_accessed=1024, transcendentals=0)


def gelu_matmul(x, pieces, bias):
    rows, inner = x.shape
    tile = 512
    width = bias.shape[1]
    tiles = [item[2] // tile for item in pieces]
    specs = []
    before = 0
    for (_, first, _), count in zip(pieces, tiles):

        def place(j, first=first, before=before, count=count):
            return 0, first // tile + jnp.clip(j - before, 0, count - 1)

        specs.append(pl.BlockSpec((inner, tile), place))
        before = before + count
    out = pl.BlockSpec((rows, tile), lambda j: (0, j))
    return pl.pallas_call(
        functools.partial(gelu_matmul_kernel, rows // 4, tiles),
        out_shape=(jax.ShapeDtypeStruct((rows, width), BF),) * 2,
        grid=(width // tile,),
        in_specs=[pl.BlockSpec((rows, inner), lambda j: (0, 0)), pl.BlockSpec((1, tile), lambda j: (0, j))] + specs,
        out_specs=(out, out),
        cost_estimate=light(),
        name="gelu_matmul",
    )(x, bias, *[item[0] for item in pieces])


def back_product_kernel(count, *refs):
    total = mm(refs[0][...], refs[count][...], NT)
    for i in range(1, count):
        total = total + mm(refs[i][...], refs[count + i][...], NT)
    refs[-1][...] = total


def back_product(pieces, weights):
    count = len(pieces)
    rows, width = pieces[0].shape
    height = weights[0].shape[0]
    tile = 512
    whole = pl.BlockSpec((rows, width), lambda j: (0, 0))
    part = pl.BlockSpec((tile, width), lambda j: (j, 0))
    return pl.pallas_call(
        functools.partial(back_product_kernel, count),
        out_shape=jax.ShapeDtypeStruct((rows, height), F32),
        grid=(height // tile,),
        in_specs=[whole] * count + [part] * count,
        out_specs=pl.BlockSpec((rows, tile), lambda j: (0, j)),
        cost_estimate=light(),
        name="back_product",
    )(*pieces, *weights)


def slope_matmul(x, w, slope):
    rows, inner = x.shape
    width = w.shape[0]
    tile = 1024
    block = pl.BlockSpec((rows, tile), lambda j: (0, j))
    return pl.pallas_call(
        functools.partial(slope_matmul_kernel, rows // 4),
        out_shape=(jax.ShapeDtypeStruct((rows, width), BF), jax.ShapeDtypeStruct((1, width), F32)),
        grid=(width // tile,),
        in_specs=[
            pl.BlockSpec((rows, inner), lambda j: (0, 0)),
            pl.BlockSpec((tile, inner), lambda j: (j, 0)),
            block,
        ],
        out_specs=(block, pl.BlockSpec((1, tile), lambda j: (0, j))),
        cost_estimate=light(),
        name="slope_matmul",
    )(x, w, slope)


def head_lanes(shape, head):
    return (lax.broadcasted_iota(jnp.int32, shape, 1) // HD) == head


def key_mask(scores, length):
    return jnp.where(lax.broadcasted_iota(jnp.int32, scores.shape, 0) < length, scores, -1e30)


def attention_forward_kernel(slots, len_ref, q_ref, k_ref, v_ref, o_ref, lse_ref):
    length = len_ref[pl.program_id(0)]

    def attend(rows, masked):
        for pair in range(PAIRS):
            lanes = pl.ds(pair * PAIR, PAIR)
            q = q_ref[:rows, lanes]
            k = k_ref[:rows, lanes]
            v_t = v_ref[:rows, lanes].T
            outs = []
            for head in range(2):
                q_one = jnp.where(head_lanes(q.shape, head), q, jnp.zeros_like(q))
                scores = mm(k, q_one, NT)
                if masked:
                    scores = key_mask(scores, length)
                top = jnp.max(scores, axis=0, keepdims=True)
                probs = jnp.exp2((scores - top) * (SCALE * LOG2E))
                total = jnp.sum(probs, axis=0, keepdims=True)
                out = mm(v_t[head * HD : (head + 1) * HD], probs.astype(BF), NN)
                outs.append(out * (1.0 / total))
                lse_ref[0, pair * 2 + head : pair * 2 + head + 1, :rows] = top * (
                    SCALE * LOG2E
                ) + jnp.log2(total)
            o_ref[:rows, lanes] = jnp.concatenate(outs, 0).astype(BF).T

    @pl.when(length > SHORT_ROWS)
    def _():
        attend(slots, False)

    @pl.when(length <= SHORT_ROWS)
    def _():
        o_ref[...] = jnp.zeros_like(o_ref)
        lse_ref[...] = jnp.zeros_like(lse_ref)
        attend(SHORT_ROWS, True)


def attention_backward_kernel(
    slots, image, len_ref, q_ref, k_ref, v_ref, o_ref, do_ref, lse_ref, dq_ref, dk_ref, dv_ref
):
    length = len_ref[image]

    def attend(rows, masked):
        for pair in range(PAIRS):
            lanes = pl.ds(pair * PAIR, PAIR)
            q = q_ref[:rows, lanes]
            k = k_ref[:rows, lanes]
            v = v_ref[:rows, lanes]
            do = do_ref[:rows, lanes]
            weighted = o_ref[:rows, lanes].astype(F32) * do.astype(F32)
            k_t = k.T
            zero = jnp.zeros_like(q)
            dqs = []
            dks = []
            dvs = []
            for head in range(2):
                own = head_lanes(q.shape, head)
                ones = jnp.where(head_lanes((8, PAIR), head), 1.0, 0.0)
                row_dot = lax.dot_general(
                    ones, weighted, NT, precision=lax.Precision.HIGHEST, preferred_element_type=F32
                )[0:1]
                scores = mm(k, jnp.where(own, q, zero), NT)
                if masked:
                    scores = key_mask(scores, length)
                lse = lse_ref[0, pair * 2 + head : pair * 2 + head + 1, :rows]
                probs = jnp.exp2(scores * (SCALE * LOG2E) - lse)
                d_probs = mm(v, jnp.where(own, do, zero), NT)
                d_scores = (probs * (d_probs - row_dot)).astype(BF)
                dvs.append(mm(probs.astype(BF), do, NN))
                dks.append(mm(d_scores, q, NN))
                dqs.append(mm(k_t[head * HD : (head + 1) * HD], d_scores, NN))
            low = head_lanes(dks[0].shape, 0)
            dv_ref[:rows, lanes] = jnp.where(low, dvs[0], dvs[1]).astype(BF)
            dk_ref[:rows, lanes] = (jnp.where(low, dks[0], dks[1]) * SCALE).astype(BF)
            dq_ref[:rows, lanes] = (jnp.concatenate(dqs, 0) * SCALE).astype(BF).T

    @pl.when(length > SHORT_ROWS)
    def _():
        attend(slots, False)

    @pl.when(length <= SHORT_ROWS)
    def _():
        for ref in (dq_ref, dk_ref, dv_ref):
            ref[...] = jnp.zeros_like(ref)
        attend(SHORT_ROWS, True)


def head_blocks(slots, image, part=0):
    first = part * (HEADS // (2 * PAIRS))
    return pl.BlockSpec((slots, PAIRS * PAIR), lambda h, lens: (image, first + h))


def lse_blocks(slots, image):
    steps = HEADS // (2 * PAIRS)
    return pl.BlockSpec((1, 2 * PAIRS, slots), lambda h, lens: (image * steps + h, 0, 0))


def held_in_place(kernel, count):
    def whole(len_ref, *refs):
        return kernel(len_ref, *refs[count:])

    return whole


def attention_forward(qkv, lengths):
    images = lengths.shape[0]
    slots = qkv.shape[0] // images
    steps = HEADS // (2 * PAIRS)

    def heads(part):
        return pl.BlockSpec((slots, PAIRS * PAIR), lambda b, h, lens: (b, part * steps + h))

    return pl.pallas_call(
        functools.partial(attention_forward_kernel, slots),
        out_shape=(
            jax.ShapeDtypeStruct((images * slots, D), BF),
            jax.ShapeDtypeStruct((images * steps, 2 * PAIRS, slots), F32),
        ),
        grid_spec=pltpu.PrefetchScalarGridSpec(
            num_scalar_prefetch=1,
            grid=(images, steps),
            in_specs=[heads(part) for part in range(3)],
            out_specs=(heads(0), pl.BlockSpec((1, 2 * PAIRS, slots), lambda b, h, lens: (b * steps + h, 0, 0))),
        ),
        cost_estimate=light(),
        name="attention_forward",
    )(lengths, qkv, qkv, qkv)


def attention_backward(image, qkv, attended, d_attended, lse, lengths, filled):
    images = lengths.shape[0]
    slots = qkv.shape[0] // images
    steps = HEADS // (2 * PAIRS)
    block = head_blocks(slots, image)
    kernel = functools.partial(attention_backward_kernel, slots, image)
    anywhere = [pl.BlockSpec(memory_space=pl.ANY)] * len(filled)
    return pl.pallas_call(
        held_in_place(kernel, len(filled)),
        out_shape=tuple(jax.ShapeDtypeStruct((images * slots, D), BF) for _ in range(3)),
        grid_spec=pltpu.PrefetchScalarGridSpec(
            num_scalar_prefetch=1,
            grid=(steps,),
            in_specs=anywhere
            + [head_blocks(slots, image, part) for part in range(3)]
            + [block] * 2
            + [lse_blocks(slots, image)],
            out_specs=(block, block, block),
        ),
        input_output_aliases={1 + i: i for i in range(len(filled))},
        cost_estimate=light(),
        name="attention_backward",
    )(lengths, *filled, qkv, qkv, qkv, attended, d_attended, lse)


def gather(shard):
    return lax.all_gather(shard, "fsdp", axis=0, tiled=True)


def scatter_sum(grad):
    return lax.psum_scatter(grad.astype(BF), "fsdp", scatter_dimension=0, tiled=True).astype(F32)


def bit_value(bit):
    return (lax.axis_index("fsdp") >> bit) & 1


def swap(value, bit):
    count = lax.axis_size("fsdp")
    return lax.ppermute(value, "fsdp", [(i, i ^ (1 << bit)) for i in range(count)])


def pick(value, axis, index):
    return lax.dynamic_index_in_dim(value, index, axis, keepdims=False)


def rotations():
    bits = (lax.axis_size("fsdp") - 1).bit_length()
    if bits == 5:
        return ((1, 2, 3, 4), (2, 3, 1, 4), (3, 1, 2, 4))
    rest = tuple(range(1, bits))
    third = max(1, len(rest) // 3)
    return (rest, rest[third:] + rest[:third], rest[2 * third :] + rest[: 2 * third])


def tie(*values):
    return lax.optimization_barrier(values)


class Gathering:
    def __init__(self, shard, order):
        self.width = shard.shape[-1]
        self.order = tuple(reversed(order)) + (0,)
        self.held = shard
        self.have = []
        self.other = None

    def send(self):
        if len(self.have) < len(self.order):
            self.other = swap(self.held, self.order[len(self.have)])

    def step(self, value):
        self.join()
        if len(self.have) < len(self.order):
            self.held, value = tie(self.held, value)
        self.send()
        return value

    def join(self):
        if self.other is None:
            return
        bit = self.order[len(self.have)]
        place = sum(1 for item in self.have if item > bit)
        shape = self.held.shape[:place] + (2,) + self.held.shape[place:]
        own = lax.broadcasted_iota(jnp.int32, shape, place) == bit_value(bit)
        self.held = jnp.where(own, jnp.expand_dims(self.held, place), jnp.expand_dims(self.other, place))
        self.have.append(bit)
        self.other = None

    def finish(self, *widths):
        mine = bit_value(0)
        outs = []
        first = 0
        for width in widths:
            columns = slice(first, first + width)
            held, other = self.held[..., columns], self.other[..., columns]
            place = len(self.have)
            shape = held.shape[:place] + (2,) + held.shape[place:]
            own = lax.broadcasted_iota(jnp.int32, shape, place) == mine
            joined = jnp.where(own, jnp.expand_dims(held, place), jnp.expand_dims(other, place))
            outs.append(joined.reshape(-1, width))
            first = first + width
        return outs


class Scattering:
    def __init__(self, grad, order):
        self.order = (0,) + tuple(order)
        self.left = sorted(self.order, reverse=True)
        self.width = grad.shape[1]
        self.parts = [grad.astype(BF).reshape((2,) * len(self.order) + (-1, self.width))]
        self.done = 0

    def split(self):
        bit = self.order[self.done]
        axis = self.left.index(bit)
        mine = bit_value(bit)
        self.keep = sum(pick(item, axis, mine).astype(F32) for item in self.parts).astype(BF)
        self.left.remove(bit)
        return sum(pick(item, axis, 1 - mine).astype(F32) for item in self.parts).astype(BF)

    def send(self, away):
        self.parts = [self.keep, swap(away, self.order[self.done])]
        self.done = self.done + 1

    def total(self):
        return sum(item.astype(F32) for item in self.parts).reshape(-1, self.width)


def scatter_step(streams, *values):
    live = [item for item in streams if item.done < len(item.order)]
    away = [item.split() for item in live]
    tied = list(tie(*away, *values))
    for item, value in zip(live, tied):
        item.send(value)
    return tied[len(live) :]


def chip_groups():
    return [[i for i in range(lax.axis_size("fsdp")) if i % 2 == c] for c in range(2)]


def chip_sum(grad):
    return lax.psum_scatter(grad, "fsdp", scatter_dimension=0, axis_index_groups=chip_groups(), tiled=True)


def advance(streams, *values):
    for item in streams:
        item.join()
    live = [item for item in streams if len(item.have) < len(item.order)]
    held = tie(*[item.held for item in live], *values)
    for item, value in zip(live, held):
        item.held = value
        item.send()
    return held[len(live) :]


def body(
    tokens,
    lengths,
    cotangent,
    ln1_gain,
    ln1_bias,
    w_qkv,
    b_qv,
    w_out,
    b_out,
    ln2_gain,
    ln2_bias,
    w_up,
    b_up,
    w_down,
    b_down,
    ln3_gain,
    ln3_bias,
    w_learn,
    b_learn,
    w_map,
):
    micro, local, slots, _ = tokens.shape
    images = micro * local
    shard_rows = w_qkv.shape[0]
    devices = D // shard_rows
    vectors = (
        ln1_gain, ln1_bias, b_out, ln2_gain, ln2_bias, b_down, ln3_gain, ln3_bias, b_learn, b_qv, b_up,
    )
    lines = jnp.concatenate([item.reshape(-1, shard_rows).T for item in vectors], axis=1)
    line_count = lines.shape[1]
    small_count = line_count + w_map.shape[1]
    pad = (-small_count) % 128
    order_x, order_y, order_z = rotations()
    small = jnp.concatenate([lines, w_map, jnp.zeros((shard_rows, pad), BF)], axis=1)
    wide = gather(jnp.concatenate([w_up, w_out, w_learn], axis=1))
    w_down = gather(w_down)
    streams = [
        Gathering(w_qkv[:, D : 2 * D], order_y),
        Gathering(w_qkv[:, 2 * D :], order_z),
        Gathering(jnp.concatenate([w_qkv[:, :D], small], axis=1), order_x),
    ]
    for _ in range(len(streams[0].order)):
        advance(streams)
    (w_k,) = streams[0].finish(D)
    (w_v,) = streams[1].finish(D)
    w_q, spread = streams[2].finish(D, small.shape[1])
    w_qkv = jnp.concatenate([w_q, w_k, w_v], axis=1)
    spread = spread[:, :small_count]
    w_out = wide[:, 4 * D : 5 * D]
    w_learn = wide[:, 5 * D :]
    lines = spread[:, :line_count].T.astype(F32)
    named = []
    offset = 0
    for item in vectors:
        count = item.shape[0] // shard_rows
        part = lines[offset : offset + count]
        if count > 1:
            part = part.reshape(count, devices, shard_rows).transpose(1, 0, 2)
        named.append(part.reshape(1, -1))
        offset = offset + count
    (ln1_gain, ln1_bias, b_out, ln2_gain, ln2_bias, b_down, ln3_gain, ln3_bias, b_learn, b_qv, b_up) = named
    w_map = spread[:, offset:]
    lengths = lengths.reshape(images)
    row_total = images * slots
    source = tokens.reshape(row_total, D).astype(F32)
    hidden = layer_norm(source, ln1_gain, ln1_bias).astype(BF)
    qkv_bias = jnp.concatenate([b_qv[:, :D], jnp.zeros((1, D), F32), b_qv[:, D:]], axis=1)
    qkv = (mm(hidden, w_qkv, NN) + qkv_bias).astype(BF)
    attended, lse = attention_forward(qkv, lengths)
    middle = source + mm(attended, w_out, NN) + b_out
    normed = layer_norm(middle, ln2_gain, ln2_bias).astype(BF)
    up_act, up_slope = gelu_matmul(normed, [(wide, 0, 4 * D)], b_up)
    output = middle + mm(up_act, w_down, NN) + b_down
    learn_in = layer_norm(output, ln3_gain, ln3_bias).astype(BF)
    learn_act, learn_slope = gelu_matmul(learn_in, [(wide, 5 * D, D)], b_learn)
    logits = mm(learn_act, w_map, NN)
    slot_valid = lax.broadcasted_iota(jnp.int32, (images, slots, 1), 1) < lengths[:, None, None]
    pool_share = (slot_valid.astype(F32) / lengths[:, None, None].astype(F32)).reshape(row_total, 1)
    squashed = jax.nn.sigmoid(logits)
    pool_maps = (squashed * pool_share).reshape(images, slots, -1)
    by_image = output.reshape(images, slots, D)
    pool_grad = cotangent.reshape(images, -1, D)
    d_maps = jnp.einsum("bsd,bmd->bsm", by_image, pool_grad, precision=lax.Precision.HIGHEST)
    d_maps = d_maps.reshape(row_total, -1)
    d_output = jnp.einsum("bsm,bmd->bsd", pool_maps, pool_grad, precision=lax.Precision.HIGHEST)
    d_output = d_output.reshape(row_total, D)
    d_logits = (d_maps * pool_share * squashed * (1.0 - squashed)).astype(BF)
    g_map = mm(learn_act, d_logits, TN)
    d_learn = (learn_slope.astype(F32) * mm(d_logits, w_map, NT)).astype(BF)
    g_blearn = jnp.sum(d_learn.astype(F32), axis=0)
    d_norm3, g_ln3, h_ln3 = norm_back(output, ln3_gain, mm(d_learn, w_learn, NT))
    d_output = d_output + d_norm3
    d_mlp = d_output.astype(BF)
    g_bdown = jnp.sum(d_mlp.astype(F32), axis=0)
    mine = bit_value(0)

    def core_parts(grad):
        blocks = grad.astype(BF).reshape(devices // 2, 2, -1, grad.shape[1])
        return pick(blocks, 1, mine), pick(blocks, 1, 1 - mine)

    def add(left, right):
        return (left.astype(F32) + right.astype(F32)).astype(BF)

    keep, away = core_parts(mm(up_act, d_mlp, TN))
    keep, away, d_learn = tie(keep, away, d_learn)
    other = swap(away, 0)
    g_wlearn = mm(learn_in, d_learn, TN).astype(BF)
    other, keep, g_wlearn, d_mlp = tie(other, keep, g_wlearn, d_mlp)
    g_down = add(keep, other)
    g_down, d_mlp = tie(g_down, d_mlp)
    g_wdown = chip_sum(g_down.reshape(-1, D)).astype(F32)
    d_up, g_bup = slope_matmul(d_mlp, w_down, up_slope)
    up_keep, up_away = core_parts(mm(normed, d_up, TN))
    up_keep, up_away, d_up = tie(up_keep, up_away, d_up)
    up_other = swap(up_away, 0)
    d_normed = back_product([d_up], [wide])
    d_norm2, g_ln2, h_ln2 = norm_back(middle, ln2_gain, d_normed)
    d_middle = d_output + d_norm2
    d_branch = d_middle.astype(BF)
    g_bout = jnp.sum(d_branch.astype(F32), axis=0)
    out_stream = Scattering(jnp.concatenate([mm(attended, d_branch, TN).astype(BF), g_wlearn], axis=1), order_y)
    d_attended = mm(d_branch, w_out, NT).astype(BF)
    (d_attended,) = scatter_step([out_stream], d_attended)
    filled = attention_backward(0, qkv, attended, d_attended, lse, lengths, ())
    up_other, up_keep, *filled = scatter_step([out_stream], up_other, up_keep, *filled)
    g_up = add(up_keep, up_other)
    g_up, *filled = tie(g_up, *filled)
    g_wup = chip_sum(g_up.reshape(-1, g_up.shape[-1])).astype(F32)
    for image in range(1, images):
        filled = attention_backward(image, qkv, attended, d_attended, lse, lengths, filled)
    filled = scatter_step([out_stream], *filled)
    late = []
    parts = list(filled)
    for n, order in enumerate((order_x, order_y, order_z)):
        stream = Scattering(mm(hidden, parts[n], TN), order)
        parts = scatter_step([stream], *parts)
        late.append(stream)
    g_bqv = jnp.concatenate([jnp.sum(item.astype(F32), axis=0) for item in (parts[0], parts[2])])
    g_bqv, *parts = scatter_step(late, g_bqv, *parts)
    d_hidden = back_product(parts, [w_q, w_k, w_v])
    d_norm1, g_ln1, h_ln1 = norm_back(source, ln1_gain, d_hidden)
    grads = (g_ln1, h_ln1, g_bout, g_ln2, h_ln2, g_bdown, g_ln3, h_ln3, g_blearn, g_bqv, g_bup)
    lines = jnp.concatenate(
        [item.reshape(devices, -1, shard_rows).transpose(1, 0, 2).reshape(-1, D) for item in grads], axis=0
    )
    spread = jnp.concatenate([lines.T, g_map, jnp.zeros((D, pad), F32)], axis=1)
    small = Scattering(spread, order_z)
    scatter_step([small])
    d_image = (d_middle + d_norm1).reshape(tokens.shape)
    by_image, d_image = tie(by_image, d_image)
    pooled = jnp.einsum("bsm,bsd->bmd", pool_maps, by_image, precision=lax.Precision.HIGHEST)
    for step in range(len(small.order)):
        (d_image,) = scatter_step(late + [out_stream], d_image)
        if step == 2:
            (pooled,) = scatter_step([small], pooled)
        else:
            scatter_step([small])
    g_wqkv = jnp.concatenate([item.total() for item in late], axis=1)
    small = small.total()
    joint = out_stream.total()
    g_wout = joint[:, :D]
    g_wlearn = joint[:, D:]
    outs = []
    offset = 0
    for item in vectors:
        count = item.shape[0] // shard_rows
        outs.append(small[:, offset : offset + count].T.reshape(-1))
        offset = offset + count
    (g_ln1, h_ln1, g_bout, g_ln2, h_ln2, g_bdown, g_ln3, h_ln3, g_blearn, g_bqv, g_bup) = outs
    g_map = small[:, offset:small_count]
    pooled = pooled.reshape(cotangent.shape)
    return (
        pooled, d_image, g_ln1, h_ln1, g_wqkv, g_bqv, g_wout, g_bout, g_ln2, h_ln2,
        g_wup, g_bup, g_wdown, g_bdown, g_ln3, h_ln3, g_wlearn, g_blearn, g_map,
    )


def solution(mesh):
    rows = P("fsdp", None)
    line = P("fsdp")
    batch = P(None, "fsdp", None, None)
    params = (line, line, rows, line, rows, line, line, line, rows, line, rows, line, line, line, rows, line, rows)
    return jax.shard_map(
        body,
        mesh=mesh,
        in_specs=(batch, P(None, "fsdp"), batch) + params,
        out_specs=(batch, batch) + params,
        check_vma=False,
    )
```

```python
import functools

import jax
import jax.numpy as jnp
from jax import lax
from jax.experimental import pallas as pl
from jax.experimental.pallas import tpu as pltpu
from jax.sharding import PartitionSpec as P

D = 1024
HEADS = 16
HD = 64
PAIR = 2 * HD
EPSILON = 1e-06
SCALE = 0.125
LOG2E = 1.4426950408889634
SHORT_ROWS = 256
PAIRS = 2
BF = jnp.bfloat16
F32 = jnp.float32

NN = (((1,), (0,)), ((), ()))
NT = (((1,), (1,)), ((), ()))
TN = (((0,), (0,)), ((), ()))


def mm(left, right, dims):
    return lax.dot_general(left, right, dims, preferred_element_type=F32)


def layer_norm_parts(values):
    row_mean = jnp.mean(values, axis=-1, keepdims=True)
    centered = values - row_mean
    variance = jnp.mean(centered * centered, axis=-1, keepdims=True)
    rstd = lax.rsqrt(variance + EPSILON)
    return centered * rstd, rstd


def layer_norm(values, gain, shift):
    return layer_norm_parts(values)[0] * gain + shift


def norm_back(values, gain, incoming):
    normed, rstd = layer_norm_parts(values)
    scaled = incoming * gain
    grad = rstd * (
        scaled
        - jnp.mean(scaled, axis=-1, keepdims=True)
        - normed * jnp.mean(scaled * normed, axis=-1, keepdims=True)
    )
    return grad, jnp.sum(incoming * normed, axis=0), jnp.sum(incoming, axis=0)


ERFCX = (
    0.18636609783492827,
    0.1828374067871815,
    0.2019228837403338,
    0.045013532984771946,
    0.4125364399329413,
    -0.3554335531070661,
    0.46268519224041466,
    -0.13592808196895617,
)
ERFCX_SCALE = 0.33


def gelu_with_slope(values):
    near = 1.0 / (1.0 + jnp.abs(values) * (ERFCX_SCALE * 0.5**0.5))
    series = 0.5 * ERFCX[-1] * near + 0.5 * ERFCX[-2]
    for item in ERFCX[-3::-1]:
        series = series * near + 0.5 * item
    bell = jnp.exp2((values * values) * (-0.5 * LOG2E))
    tail = (bell * near) * series
    half = jnp.where(values < 0, tail, 1.0 - tail)
    return values * half, half + values * (bell * 0.3989422804014327)


def gelu_matmul_kernel(chunk, tiles, x_ref, b_ref, *refs):
    w_refs = refs[: len(tiles)]
    act_ref, slope_ref = refs[len(tiles) :]
    step = pl.program_id(0)
    first = 0
    for w_ref, count in zip(w_refs, tiles):

        @pl.when((step >= first) & (step < first + count))
        def _(w_ref=w_ref):
            for start in range(0, x_ref.shape[0], chunk):
                rows = pl.ds(start, chunk)
                act, slope = gelu_with_slope(mm(x_ref[rows], w_ref[...], NN) + b_ref[...])
                act_ref[rows] = act.astype(BF)
                slope_ref[rows] = slope.astype(BF)

        first = first + count


def slope_matmul_kernel(chunk, x_ref, w_ref, slope_ref, out_ref, sum_ref):
    total = jnp.zeros(sum_ref.shape, F32)
    for start in range(0, x_ref.shape[0], chunk):
        rows = pl.ds(start, chunk)
        out = (mm(x_ref[rows], w_ref[...], NT) * slope_ref[rows].astype(F32)).astype(BF)
        out_ref[rows] = out
        total = total + jnp.sum(out.astype(F32), axis=0, keepdims=True)
    sum_ref[...] = total


def light():
    return pl.CostEstimate(flops=1024, bytes_accessed=1024, transcendentals=0)


def gelu_matmul(x, pieces, bias):
    rows, inner = x.shape
    tile = 512
    width = bias.shape[1]
    tiles = [item[2] // tile for item in pieces]
    specs = []
    before = 0
    for (_, first, _), count in zip(pieces, tiles):

        def place(j, first=first, before=before, count=count):
            return 0, first // tile + jnp.clip(j - before, 0, count - 1)

        specs.append(pl.BlockSpec((inner, tile), place))
        before = before + count
    out = pl.BlockSpec((rows, tile), lambda j: (0, j))
    return pl.pallas_call(
        functools.partial(gelu_matmul_kernel, rows // 4, tiles),
        out_shape=(jax.ShapeDtypeStruct((rows, width), BF),) * 2,
        grid=(width // tile,),
        in_specs=[pl.BlockSpec((rows, inner), lambda j: (0, 0)), pl.BlockSpec((1, tile), lambda j: (0, j))] + specs,
        out_specs=(out, out),
        cost_estimate=light(),
        name="gelu_matmul",
    )(x, bias, *[item[0] for item in pieces])


def back_product_kernel(count, *refs):
    total = mm(refs[0][...], refs[count][...], NT)
    for i in range(1, count):
        total = total + mm(refs[i][...], refs[count + i][...], NT)
    refs[-1][...] = total


def back_product(pieces, weights):
    count = len(pieces)
    rows, width = pieces[0].shape
    height = weights[0].shape[0]
    tile = 512
    whole = pl.BlockSpec((rows, width), lambda j: (0, 0))
    part = pl.BlockSpec((tile, width), lambda j: (j, 0))
    return pl.pallas_call(
        functools.partial(back_product_kernel, count),
        out_shape=jax.ShapeDtypeStruct((rows, height), F32),
        grid=(height // tile,),
        in_specs=[whole] * count + [part] * count,
        out_specs=pl.BlockSpec((rows, tile), lambda j: (0, j)),
        cost_estimate=light(),
        name="back_product",
    )(*pieces, *weights)


def slope_matmul(x, w, slope):
    rows, inner = x.shape
    width = w.shape[0]
    tile = 1024
    block = pl.BlockSpec((rows, tile), lambda j: (0, j))
    return pl.pallas_call(
        functools.partial(slope_matmul_kernel, rows // 4),
        out_shape=(jax.ShapeDtypeStruct((rows, width), BF), jax.ShapeDtypeStruct((1, width), F32)),
        grid=(width // tile,),
        in_specs=[
            pl.BlockSpec((rows, inner), lambda j: (0, 0)),
            pl.BlockSpec((tile, inner), lambda j: (j, 0)),
            block,
        ],
        out_specs=(block, pl.BlockSpec((1, tile), lambda j: (0, j))),
        cost_estimate=light(),
        name="slope_matmul",
    )(x, w, slope)


def head_lanes(shape, head):
    return (lax.broadcasted_iota(jnp.int32, shape, 1) // HD) == head


def key_mask(scores, length):
    return jnp.where(lax.broadcasted_iota(jnp.int32, scores.shape, 0) < length, scores, -1e30)


def attention_forward_kernel(slots, len_ref, q_ref, k_ref, v_ref, o_ref, lse_ref):
    length = len_ref[pl.program_id(0)]

    def attend(rows, masked):
        for pair in range(PAIRS):
            lanes = pl.ds(pair * PAIR, PAIR)
            q = q_ref[:rows, lanes]
            k = k_ref[:rows, lanes]
            v_t = v_ref[:rows, lanes].T
            outs = []
            for head in range(2):
                q_one = jnp.where(head_lanes(q.shape, head), q, jnp.zeros_like(q))
                scores = mm(k, q_one, NT)
                if masked:
                    scores = key_mask(scores, length)
                top = jnp.max(scores, axis=0, keepdims=True)
                probs = jnp.exp2((scores - top) * (SCALE * LOG2E))
                total = jnp.sum(probs, axis=0, keepdims=True)
                out = mm(v_t[head * HD : (head + 1) * HD], probs.astype(BF), NN)
                outs.append(out * (1.0 / total))
                lse_ref[0, pair * 2 + head : pair * 2 + head + 1, :rows] = top * (
                    SCALE * LOG2E
                ) + jnp.log2(total)
            o_ref[:rows, lanes] = jnp.concatenate(outs, 0).astype(BF).T

    @pl.when(length > SHORT_ROWS)
    def _():
        attend(slots, False)

    @pl.when(length <= SHORT_ROWS)
    def _():
        o_ref[...] = jnp.zeros_like(o_ref)
        lse_ref[...] = jnp.zeros_like(lse_ref)
        attend(SHORT_ROWS, True)


def attention_backward_kernel(
    slots, image, len_ref, q_ref, k_ref, v_ref, o_ref, do_ref, lse_ref, dq_ref, dk_ref, dv_ref
):
    length = len_ref[image]

    def attend(rows, masked):
        for pair in range(PAIRS):
            lanes = pl.ds(pair * PAIR, PAIR)
            q = q_ref[:rows, lanes]
            k = k_ref[:rows, lanes]
            v = v_ref[:rows, lanes]
            do = do_ref[:rows, lanes]
            weighted = o_ref[:rows, lanes].astype(F32) * do.astype(F32)
            k_t = k.T
            zero = jnp.zeros_like(q)
            dqs = []
            dks = []
            dvs = []
            for head in range(2):
                own = head_lanes(q.shape, head)
                ones = jnp.where(head_lanes((8, PAIR), head), 1.0, 0.0)
                row_dot = lax.dot_general(
                    ones, weighted, NT, precision=lax.Precision.HIGHEST, preferred_element_type=F32
                )[0:1]
                scores = mm(k, jnp.where(own, q, zero), NT)
                if masked:
                    scores = key_mask(scores, length)
                lse = lse_ref[0, pair * 2 + head : pair * 2 + head + 1, :rows]
                probs = jnp.exp2(scores * (SCALE * LOG2E) - lse)
                d_probs = mm(v, jnp.where(own, do, zero), NT)
                d_scores = (probs * (d_probs - row_dot)).astype(BF)
                dvs.append(mm(probs.astype(BF), do, NN))
                dks.append(mm(d_scores, q, NN))
                dqs.append(mm(k_t[head * HD : (head + 1) * HD], d_scores, NN))
            low = head_lanes(dks[0].shape, 0)
            dv_ref[:rows, lanes] = jnp.where(low, dvs[0], dvs[1]).astype(BF)
            dk_ref[:rows, lanes] = (jnp.where(low, dks[0], dks[1]) * SCALE).astype(BF)
            dq_ref[:rows, lanes] = (jnp.concatenate(dqs, 0) * SCALE).astype(BF).T

    @pl.when(length > SHORT_ROWS)
    def _():
        attend(slots, False)

    @pl.when(length <= SHORT_ROWS)
    def _():
        for ref in (dq_ref, dk_ref, dv_ref):
            ref[...] = jnp.zeros_like(ref)
        attend(SHORT_ROWS, True)


def head_blocks(slots, image, part=0):
    first = part * (HEADS // (2 * PAIRS))
    return pl.BlockSpec((slots, PAIRS * PAIR), lambda h, lens: (image, first + h))


def lse_blocks(slots, image):
    steps = HEADS // (2 * PAIRS)
    return pl.BlockSpec((1, 2 * PAIRS, slots), lambda h, lens: (image * steps + h, 0, 0))


def held_in_place(kernel, count):
    def whole(len_ref, *refs):
        return kernel(len_ref, *refs[count:])

    return whole


def attention_forward(qkv, lengths):
    images = lengths.shape[0]
    slots = qkv.shape[0] // images
    steps = HEADS // (2 * PAIRS)

    def heads(part):
        return pl.BlockSpec((slots, PAIRS * PAIR), lambda b, h, lens: (b, part * steps + h))

    return pl.pallas_call(
        functools.partial(attention_forward_kernel, slots),
        out_shape=(
            jax.ShapeDtypeStruct((images * slots, D), BF),
            jax.ShapeDtypeStruct((images * steps, 2 * PAIRS, slots), F32),
        ),
        grid_spec=pltpu.PrefetchScalarGridSpec(
            num_scalar_prefetch=1,
            grid=(images, steps),
            in_specs=[heads(part) for part in range(3)],
            out_specs=(heads(0), pl.BlockSpec((1, 2 * PAIRS, slots), lambda b, h, lens: (b * steps + h, 0, 0))),
        ),
        cost_estimate=light(),
        name="attention_forward",
    )(lengths, qkv, qkv, qkv)


def attention_backward(image, qkv, attended, d_attended, lse, lengths, filled):
    images = lengths.shape[0]
    slots = qkv.shape[0] // images
    steps = HEADS // (2 * PAIRS)
    block = head_blocks(slots, image)
    kernel = functools.partial(attention_backward_kernel, slots, image)
    anywhere = [pl.BlockSpec(memory_space=pl.ANY)] * len(filled)
    return pl.pallas_call(
        held_in_place(kernel, len(filled)),
        out_shape=tuple(jax.ShapeDtypeStruct((images * slots, D), BF) for _ in range(3)),
        grid_spec=pltpu.PrefetchScalarGridSpec(
            num_scalar_prefetch=1,
            grid=(steps,),
            in_specs=anywhere
            + [head_blocks(slots, image, part) for part in range(3)]
            + [block] * 2
            + [lse_blocks(slots, image)],
            out_specs=(block, block, block),
        ),
        input_output_aliases={1 + i: i for i in range(len(filled))},
        cost_estimate=light(),
        name="attention_backward",
    )(lengths, *filled, qkv, qkv, qkv, attended, d_attended, lse)


def gather(shard):
    return lax.all_gather(shard, "fsdp", axis=0, tiled=True)


def scatter_sum(grad):
    return lax.psum_scatter(grad.astype(BF), "fsdp", scatter_dimension=0, tiled=True).astype(F32)


def bit_value(bit):
    return (lax.axis_index("fsdp") >> bit) & 1


def swap(value, bit):
    count = lax.axis_size("fsdp")
    return lax.ppermute(value, "fsdp", [(i, i ^ (1 << bit)) for i in range(count)])


def pick(value, axis, index):
    return lax.dynamic_index_in_dim(value, index, axis, keepdims=False)


def rotations():
    bits = (lax.axis_size("fsdp") - 1).bit_length()
    if bits == 5:
        return ((1, 2, 3, 4), (2, 3, 1, 4), (3, 1, 2, 4))
    rest = tuple(range(1, bits))
    third = max(1, len(rest) // 3)
    return (rest, rest[third:] + rest[:third], rest[2 * third :] + rest[: 2 * third])


def tie(*values):
    return lax.optimization_barrier(values)


class Gathering:
    def __init__(self, shard, order):
        self.width = shard.shape[-1]
        self.order = tuple(reversed(order)) + (0,)
        self.held = shard
        self.have = []
        self.other = None

    def send(self):
        if len(self.have) < len(self.order):
            self.other = swap(self.held, self.order[len(self.have)])

    def step(self, value):
        self.join()
        if len(self.have) < len(self.order):
            self.held, value = tie(self.held, value)
        self.send()
        return value

    def join(self):
        if self.other is None:
            return
        bit = self.order[len(self.have)]
        place = sum(1 for item in self.have if item > bit)
        shape = self.held.shape[:place] + (2,) + self.held.shape[place:]
        own = lax.broadcasted_iota(jnp.int32, shape, place) == bit_value(bit)
        self.held = jnp.where(own, jnp.expand_dims(self.held, place), jnp.expand_dims(self.other, place))
        self.have.append(bit)
        self.other = None

    def finish(self, *widths):
        mine = bit_value(0)
        outs = []
        first = 0
        for width in widths:
            columns = slice(first, first + width)
            held, other = self.held[..., columns], self.other[..., columns]
            place = len(self.have)
            shape = held.shape[:place] + (2,) + held.shape[place:]
            own = lax.broadcasted_iota(jnp.int32, shape, place) == mine
            joined = jnp.where(own, jnp.expand_dims(held, place), jnp.expand_dims(other, place))
            outs.append(joined.reshape(-1, width))
            first = first + width
        return outs


class Scattering:
    def __init__(self, grad, order):
        self.order = (0,) + tuple(order)
        self.left = sorted(self.order, reverse=True)
        self.width = grad.shape[1]
        self.parts = [grad.astype(BF).reshape((2,) * len(self.order) + (-1, self.width))]
        self.done = 0

    def split(self):
        bit = self.order[self.done]
        axis = self.left.index(bit)
        mine = bit_value(bit)
        self.keep = sum(pick(item, axis, mine).astype(F32) for item in self.parts).astype(BF)
        self.left.remove(bit)
        return sum(pick(item, axis, 1 - mine).astype(F32) for item in self.parts).astype(BF)

    def send(self, away):
        self.parts = [self.keep, swap(away, self.order[self.done])]
        self.done = self.done + 1

    def total(self):
        return sum(item.astype(F32) for item in self.parts).reshape(-1, self.width)


def scatter_step(streams, *values):
    live = [item for item in streams if item.done < len(item.order)]
    away = [item.split() for item in live]
    tied = list(tie(*away, *values))
    for item, value in zip(live, tied):
        item.send(value)
    return tied[len(live) :]


def chip_groups():
    return [[i for i in range(lax.axis_size("fsdp")) if i % 2 == c] for c in range(2)]


def chip_sum(grad):
    return lax.psum_scatter(grad, "fsdp", scatter_dimension=0, axis_index_groups=chip_groups(), tiled=True)


def advance(streams, *values):
    for item in streams:
        item.join()
    live = [item for item in streams if len(item.have) < len(item.order)]
    held = tie(*[item.held for item in live], *values)
    for item, value in zip(live, held):
        item.held = value
        item.send()
    return held[len(live) :]


def body(
    tokens,
    lengths,
    cotangent,
    ln1_gain,
    ln1_bias,
    w_qkv,
    b_qv,
    w_out,
    b_out,
    ln2_gain,
    ln2_bias,
    w_up,
    b_up,
    w_down,
    b_down,
    ln3_gain,
    ln3_bias,
    w_learn,
    b_learn,
    w_map,
):
    micro, local, slots, _ = tokens.shape
    images = micro * local
    shard_rows = w_qkv.shape[0]
    devices = D // shard_rows
    vectors = (
        ln1_gain, ln1_bias, b_out, ln2_gain, ln2_bias, b_down, ln3_gain, ln3_bias, b_learn, b_qv, b_up,
    )
    lines = jnp.concatenate([item.reshape(-1, shard_rows).T for item in vectors], axis=1)
    line_count = lines.shape[1]
    small_count = line_count + w_map.shape[1]
    pad = (-small_count) % 128
    order_x, order_y, order_z = rotations()
    small = jnp.concatenate([lines, w_map, jnp.zeros((shard_rows, pad), BF)], axis=1)
    wide = gather(jnp.concatenate([w_up, w_out, w_learn], axis=1))
    w_down = gather(w_down)
    streams = [
        Gathering(w_qkv[:, D : 2 * D], order_y),
        Gathering(w_qkv[:, 2 * D :], order_z),
        Gathering(jnp.concatenate([w_qkv[:, :D], small], axis=1), order_x),
    ]
    for _ in range(len(streams[0].order)):
        advance(streams)
    (w_k,) = streams[0].finish(D)
    (w_v,) = streams[1].finish(D)
    w_q, spread = streams[2].finish(D, small.shape[1])
    w_qkv = jnp.concatenate([w_q, w_k, w_v], axis=1)
    spread = spread[:, :small_count]
    w_out = wide[:, 4 * D : 5 * D]
    w_learn = wide[:, 5 * D :]
    lines = spread[:, :line_count].T.astype(F32)
    named = []
    offset = 0
    for item in vectors:
        count = item.shape[0] // shard_rows
        part = lines[offset : offset + count]
        if count > 1:
            part = part.reshape(count, devices, shard_rows).transpose(1, 0, 2)
        named.append(part.reshape(1, -1))
        offset = offset + count
    (ln1_gain, ln1_bias, b_out, ln2_gain, ln2_bias, b_down, ln3_gain, ln3_bias, b_learn, b_qv, b_up) = named
    w_map = spread[:, offset:]
    lengths = lengths.reshape(images)
    row_total = images * slots
    source = tokens.reshape(row_total, D).astype(F32)
    hidden = layer_norm(source, ln1_gain, ln1_bias).astype(BF)
    qkv_bias = jnp.concatenate([b_qv[:, :D], jnp.zeros((1, D), F32), b_qv[:, D:]], axis=1)
    qkv = (mm(hidden, w_qkv, NN) + qkv_bias).astype(BF)
    attended, lse = attention_forward(qkv, lengths)
    middle = source + mm(attended, w_out, NN) + b_out
    normed = layer_norm(middle, ln2_gain, ln2_bias).astype(BF)
    up_act, up_slope = gelu_matmul(normed, [(wide, 0, 4 * D)], b_up)
    output = middle + mm(up_act, w_down, NN) + b_down
    learn_in = layer_norm(output, ln3_gain, ln3_bias).astype(BF)
    learn_act, learn_slope = gelu_matmul(learn_in, [(wide, 5 * D, D)], b_learn)
    logits = mm(learn_act, w_map, NN)
    slot_valid = lax.broadcasted_iota(jnp.int32, (images, slots, 1), 1) < lengths[:, None, None]
    pool_share = (slot_valid.astype(F32) / lengths[:, None, None].astype(F32)).reshape(row_total, 1)
    squashed = jax.nn.sigmoid(logits)
    pool_maps = (squashed * pool_share).reshape(images, slots, -1)
    by_image = output.reshape(images, slots, D)
    pool_grad = cotangent.reshape(images, -1, D)
    d_maps = jnp.einsum("bsd,bmd->bsm", by_image, pool_grad, precision=lax.Precision.HIGHEST)
    d_maps = d_maps.reshape(row_total, -1)
    d_output = jnp.einsum("bsm,bmd->bsd", pool_maps, pool_grad, precision=lax.Precision.HIGHEST)
    d_output = d_output.reshape(row_total, D)
    d_logits = (d_maps * pool_share * squashed * (1.0 - squashed)).astype(BF)
    g_map = mm(learn_act, d_logits, TN)
    d_learn = (learn_slope.astype(F32) * mm(d_logits, w_map, NT)).astype(BF)
    g_blearn = jnp.sum(d_learn.astype(F32), axis=0)
    d_norm3, g_ln3, h_ln3 = norm_back(output, ln3_gain, mm(d_learn, w_learn, NT))
    d_output = d_output + d_norm3
    d_mlp = d_output.astype(BF)
    g_bdown = jnp.sum(d_mlp.astype(F32), axis=0)
    mine = bit_value(0)

    def core_parts(grad):
        blocks = grad.astype(BF).reshape(devices // 2, 2, -1, grad.shape[1])
        return pick(blocks, 1, mine), pick(blocks, 1, 1 - mine)

    def add(left, right):
        return (left.astype(F32) + right.astype(F32)).astype(BF)

    keep, away = core_parts(mm(up_act, d_mlp, TN))
    keep, away, d_learn = tie(keep, away, d_learn)
    other = swap(away, 0)
    g_wlearn = mm(learn_in, d_learn, TN).astype(BF)
    other, keep, g_wlearn, d_mlp = tie(other, keep, g_wlearn, d_mlp)
    g_down = add(keep, other)
    g_down, d_mlp = tie(g_down, d_mlp)
    g_wdown = chip_sum(g_down.reshape(-1, D)).astype(F32)
    d_up, g_bup = slope_matmul(d_mlp, w_down, up_slope)
    up_keep, up_away = core_parts(mm(normed, d_up, TN))
    up_keep, up_away, d_up = tie(up_keep, up_away, d_up)
    up_other = swap(up_away, 0)
    d_normed = back_product([d_up], [wide])
    d_norm2, g_ln2, h_ln2 = norm_back(middle, ln2_gain, d_normed)
    d_middle = d_output + d_norm2
    d_branch = d_middle.astype(BF)
    g_bout = jnp.sum(d_branch.astype(F32), axis=0)
    out_stream = Scattering(jnp.concatenate([mm(attended, d_branch, TN).astype(BF), g_wlearn], axis=1), order_y)
    d_attended = mm(d_branch, w_out, NT).astype(BF)
    (d_attended,) = scatter_step([out_stream], d_attended)
    filled = attention_backward(0, qkv, attended, d_attended, lse, lengths, ())
    up_other, up_keep, *filled = scatter_step([out_stream], up_other, up_keep, *filled)
    g_up = add(up_keep, up_other)
    g_up, *filled = tie(g_up, *filled)
    g_wup = chip_sum(g_up.reshape(-1, g_up.shape[-1])).astype(F32)
    for image in range(1, images):
        filled = attention_backward(image, qkv, attended, d_attended, lse, lengths, filled)
    filled = scatter_step([out_stream], *filled)
    late = []
    parts = list(filled)
    for n, order in enumerate((order_x, order_y, order_z)):
        stream = Scattering(mm(hidden, parts[n], TN), order)
        parts = scatter_step([stream], *parts)
        late.append(stream)
    g_bqv = jnp.concatenate([jnp.sum(item.astype(F32), axis=0) for item in (parts[0], parts[2])])
    g_bqv, *parts = scatter_step(late, g_bqv, *parts)
    d_hidden = back_product(parts, [w_q, w_k, w_v])
    d_norm1, g_ln1, h_ln1 = norm_back(source, ln1_gain, d_hidden)
    grads = (g_ln1, h_ln1, g_bout, g_ln2, h_ln2, g_bdown, g_ln3, h_ln3, g_blearn, g_bqv, g_bup)
    lines = jnp.concatenate(
        [item.reshape(devices, -1, shard_rows).transpose(1, 0, 2).reshape(-1, D) for item in grads], axis=0
    )
    spread = jnp.concatenate([lines.T, g_map, jnp.zeros((D, pad), F32)], axis=1)
    small = Scattering(spread, order_z)
    scatter_step([small])
    d_image = (d_middle + d_norm1).reshape(tokens.shape)
    by_image, d_image = tie(by_image, d_image)
    pooled = jnp.einsum("bsm,bsd->bmd", pool_maps, by_image, precision=lax.Precision.HIGHEST)
    for step in range(len(small.order)):
        (d_image,) = scatter_step(late + [out_stream], d_image)
        if step == 2:
            pooled, g_wdown = scatter_step([small], pooled, g_wdown)
        else:
            scatter_step([small])
    g_wqkv = jnp.concatenate([item.total() for item in late], axis=1)
    small = small.total()
    joint = out_stream.total()
    g_wout = joint[:, :D]
    g_wlearn = joint[:, D:]
    outs = []
    offset = 0
    for item in vectors:
        count = item.shape[0] // shard_rows
        outs.append(small[:, offset : offset + count].T.reshape(-1))
        offset = offset + count
    (g_ln1, h_ln1, g_bout, g_ln2, h_ln2, g_bdown, g_ln3, h_ln3, g_blearn, g_bqv, g_bup) = outs
    g_map = small[:, offset:small_count]
    pooled = pooled.reshape(cotangent.shape)
    return (
        pooled, d_image, g_ln1, h_ln1, g_wqkv, g_bqv, g_wout, g_bout, g_ln2, h_ln2,
        g_wup, g_bup, g_wdown, g_bdown, g_ln3, h_ln3, g_wlearn, g_blearn, g_map,
    )


def solution(mesh):
    rows = P("fsdp", None)
    line = P("fsdp")
    batch = P(None, "fsdp", None, None)
    params = (line, line, rows, line, rows, line, line, line, rows, line, rows, line, line, line, rows, line, rows)
    return jax.shard_map(
        body,
        mesh=mesh,
        in_specs=(batch, P(None, "fsdp"), batch) + params,
        out_specs=(batch, batch) + params,
        check_vma=False,
    )
```
